32 devices in a mesh: ctx: 4 (over z), fsdp: 8 (over y, x, core).
Axes of the slice: x: 2, y: 2, z: 4, core: 2. Of those that a mesh axis runs over, the one named last changes fastest.
Arguments:
- tokens: bfloat16 [8, 1024, 1536], P('fsdp', 'ctx'), may hold values from -6 to 6
- cotangent: bfloat16 [8, 1024, 1536], P('fsdp', 'ctx'), may hold values from -6 to 6
- doc_ids: int32 [8, 1024], P('fsdp'), may hold values from 0 to 3, as said below
- block_order: int32 [4], replicated, may hold values from 0 to 3, as said below
- w_query: bfloat16 [1536, 1536], P('fsdp'), may hold values from -0.15625 to 0.15625
- w_key: bfloat16 [1536, 256], P('fsdp'), may hold values from -0.15625 to 0.15625
- w_value: bfloat16 [1536, 256], P('fsdp'), may hold values from -0.15625 to 0.15625
- w_out: bfloat16 [1536, 1536], P('fsdp'), may hold values from -0.625 to 0.625
- b_query: bfloat16 [1536], P('fsdp'), may hold values from -3 to 3
- b_key: bfloat16 [256], P('fsdp'), may hold values from -3 to 3
- b_value: bfloat16 [256], P('fsdp'), may hold values from -3 to 3
- gain_attn: bfloat16 [1536], P('fsdp'), may hold values from 0.5 to 1.5
- w_gate: bfloat16 [1536, 8960], P(None, 'fsdp'), may hold values from -0.15625 to 0.15625
- w_up: bfloat16 [1536, 8960], P(None, 'fsdp'), may hold values from -0.15625 to 0.15625
- w_down: bfloat16 [8960, 1536], P('fsdp'), may hold values from -0.0625 to 0.0625
- gain_ffn: bfloat16 [1536], P('fsdp'), may hold values from 0.5 to 1.5
Outputs:
- output: bfloat16 [8, 1024, 1536], P('fsdp', 'ctx')
- grad_tokens: bfloat16 [8, 1024, 1536], P('fsdp', 'ctx')
- grad_w_query: float32 [1536, 1536], P('fsdp')
- grad_w_key: float32 [1536, 256], P('fsdp')
- grad_w_value: float32 [1536, 256], P('fsdp')
- grad_w_out: float32 [1536, 1536], P('fsdp')
- grad_b_query: float32 [1536], P('fsdp')
- grad_b_key: float32 [256], P('fsdp')
- grad_b_value: float32 [256], P('fsdp')
- grad_gain_attn: float32 [1536], P('fsdp')
- grad_w_gate: float32 [1536, 8960], P(None, 'fsdp')
- grad_w_up: float32 [1536, 8960], P(None, 'fsdp')
- grad_w_down: float32 [8960, 1536], P('fsdp')
- grad_gain_ffn: float32 [1536], P('fsdp')
The draws below stay inside these ranges and needn't reach their ends.
Inputs may be any that keep to these rules, and one draw needn't show every extreme that they name: A permutation; context device c holds blocks block_order[c] and 7 - block_order[c] of every sequence, in that order. `doc_ids`: in order of position (see block_order) the ids of a sequence start at 0 and never fall, rising by one at each new document; every sequence holds exactly 4 documents.
All inputs are finite; a program needn't handle non-finite values.
Results may differ from the reference program's by a relative error of at most 0.024.
Values may be sent and summed in bfloat16 or wider, within the bound.
No kernel may reach another device: no remote copies, remote signals or barrier semaphores. Data moves between devices by JAX's collectives and lax.ppermute only.
A program may use at most 320 MiB of HBM per device.

```python
import jax
import jax.numpy as jnp
from jax import lax

D = 1536
HEADS = 12
KV_HEADS = 2
HEAD = 128
FF = 8960
BLK = 128
KVD = 256
LEN = 1024
SEQS = 8
N_CTX = 4


def shared_order(key):
    return jax.random.permutation(jax.random.fold_in(key, 7), N_CTX).astype(jnp.int32)


def draw_block_order(key, part):
    return shared_order(key)


def one_sequence(seq_key):
    length = 2 * BLK * N_CTX
    picked = jax.random.permutation(seq_key, length - 1)[:N_CTX - 1].astype(jnp.int32) + 1
    starts = jnp.zeros((length,), jnp.int32).at[picked].set(1)
    return jnp.cumsum(starts).astype(jnp.int32)


def draw_doc_ids(key, part):
    order = shared_order(key)
    seq_keys = jax.random.split(jax.random.fold_in(key, 11), SEQS)
    natural = jax.vmap(one_sequence)(seq_keys)
    blocks = jnp.stack([order, 2 * N_CTX - 1 - order], axis=1).reshape(-1)
    places = (blocks[:, None] * BLK + jnp.arange(BLK, dtype=jnp.int32)[None, :]).reshape(-1)
    return natural[:, places]


def draw_gain_attn(key, part):
    return jax.random.uniform(jax.random.fold_in(key, 13), (D,), jnp.float32, 0.5, 1.5).astype(jnp.bfloat16)


def levels(key, shape, shards, low, largest):
    loudness, own = 1.0, jax.random.fold_in(key, 6)
    for axis_at, blocks in shards:
        draws = jnp.exp(jax.random.uniform(jax.random.fold_in(own, axis_at), (blocks,), jnp.float32, low / len(shards), largest / len(shards)))
        loudness = loudness * jnp.repeat(draws, shape[axis_at] // blocks).reshape([-1 if axis == axis_at else 1 for axis in range(len(shape))])
    return loudness


def bell_draw(stream_key, shape, scale, limit, shards=(), kind=jnp.bfloat16):
    values = scale * jax.random.normal(stream_key, shape, jnp.float32)
    if shards:
        values = values * levels(stream_key, shape, shards, -0.22, 0.18)
    return jnp.clip(values, -limit, limit).astype(kind)


def setup_inputs(seed: int = 0) -> dict:
    key_list = jax.random.split(jax.random.key(seed), 17)
    tokens = bell_draw(key_list[0], (SEQS, LEN, D), 1.0, 6.0, ((0, 8), (1, 4)))
    cotangent = bell_draw(key_list[1], (SEQS, LEN, D), 1.0, 6.0, ((0, 8), (1, 4)))
    doc_ids = draw_doc_ids(jax.random.fold_in(key_list[16], 71), 0)
    block_order = draw_block_order(jax.random.fold_in(key_list[16], 71), 0)
    w_query = bell_draw(key_list[4], (D, D), D ** -0.5, 0.15625, ((0, 8),))
    w_key = bell_draw(key_list[5], (D, KVD), D ** -0.5, 0.15625, ((0, 8),))
    w_value = bell_draw(key_list[6], (D, KVD), D ** -0.5, 0.15625, ((0, 8),))
    w_out = bell_draw(key_list[7], (D, D), (D // 16) ** -0.5, 0.625, ((0, 8),))
    b_query = bell_draw(key_list[8], (D,), 0.5, 3.0, ((0, 8),))
    b_key = bell_draw(key_list[9], (KVD,), 0.5, 3.0, ((0, 8),))
    b_value = bell_draw(key_list[10], (KVD,), 0.5, 3.0, ((0, 8),))
    gain_attn = draw_gain_attn(jax.random.fold_in(key_list[16], 71), 0)
    w_gate = bell_draw(key_list[12], (D, FF), D ** -0.5, 0.15625, ((1, 8),))
    w_up = bell_draw(key_list[13], (D, FF), D ** -0.5, 0.15625, ((1, 8),))
    w_down = bell_draw(key_list[14], (FF, D), FF ** -0.5, 0.0625, ((0, 8),))
    gain_ffn = jnp.clip(1.0 + 0.1 * jax.random.normal(key_list[15], (D,), jnp.float32), 0.5, 1.5).astype(jnp.bfloat16)
    return dict(tokens=tokens, cotangent=cotangent, doc_ids=doc_ids, block_order=block_order, w_query=w_query, w_key=w_key, w_value=w_value, w_out=w_out, b_query=b_query, b_key=b_key, b_value=b_value, gain_attn=gain_attn, w_gate=w_gate, w_up=w_up, w_down=w_down, gain_ffn=gain_ffn)


THETA = 1000000.0
EPS = 1e-06
MASKED = -1e+30

@jax.custom_vjp
def low(v):
    return lax.optimization_barrier(v.astype(jnp.bfloat16)).astype(jnp.float32)

@jax.custom_vjp
def low_back(v):
    return v

def low_keep(v):
    return (low(v), None)

def low_pass(kept, grad):
    return (grad,)

def back_keep(v):
    return (v, None)

def back_low(kept, grad):
    return (low(grad),)
low.defvjp(low_keep, low_pass)
low_back.defvjp(back_keep, back_low)

def stored_places(block_order):
    order = block_order.astype(jnp.int32)
    blocks = jnp.stack([order, 2 * N_CTX - 1 - order], axis=1).reshape(-1)
    offsets = jnp.arange(BLK).astype(jnp.int32)
    return (blocks[:, None] * BLK + offsets[None, :]).reshape(-1).astype(jnp.int32)

def rotary_tables(places):
    half = HEAD // 2
    freqs = THETA ** (-jnp.arange(half).astype(jnp.float32) / half)
    angles = places.astype(jnp.float32)[:, None] * freqs[None, :]
    return (jnp.cos(angles), jnp.sin(angles))

def rotate(values, cosine, sine):
    half = values.shape[-1] // 2
    front = values[..., :half]
    back_half = values[..., half:]
    cosine = cosine[:, None, :]
    sine = sine[:, None, :]
    return jnp.concatenate([front * cosine - back_half * sine, back_half * cosine + front * sine], axis=-1)

def multiply(left, right):
    return jnp.dot(left, right, precision=lax.Precision.HIGHEST)

def rms_scale(hidden):
    return lax.rsqrt(lax.optimization_barrier(jnp.mean(hidden * hidden, axis=-1, keepdims=True)) + EPS)

def attention(queries, keys, values, places, docs):
    length = queries.shape[0]
    step_rows = min(512, length)
    count = length // step_rows
    grouped = queries.reshape(count, step_rows, KV_HEADS, HEADS // KV_HEADS, HEAD)
    place_blocks = places.reshape(count, step_rows)
    doc_blocks = docs.reshape(count, step_rows)
    scale = HEAD ** (-0.5)

    def one_block(item):
        query_block, place_block, doc_block = item
        raw = jnp.einsum('qkgd,lkd->kgql', query_block, keys, precision=lax.Precision.HIGHEST)
        scores = low_back(raw) * scale
        allowed = (places[None, :] <= place_block[:, None]) & (docs[None, :] == doc_block[:, None])
        scores = jnp.where(allowed[None, None], scores, MASKED)
        weights = low(jax.nn.softmax(scores, axis=-1))
        return jnp.einsum('kgql,lkd->qkgd', weights, values, precision=lax.Precision.HIGHEST)
    mixed = lax.map(jax.checkpoint(one_block), (grouped, place_blocks, doc_blocks))
    return mixed.reshape(length, HEADS * HEAD)

def layer(params, hidden, docs, places, cosine, sine):
    w_query, w_key, w_value, w_out, b_query, b_key, b_value, gain_attn, w_gate, w_up, w_down, gain_ffn = params
    length = hidden.shape[0]
    normed = low(hidden * rms_scale(hidden) * gain_attn)
    query_pre = low_back(multiply(normed, w_query) + b_query)
    key_pre = low_back(multiply(normed, w_key) + b_key)
    queries = low(rotate(query_pre.reshape(length, HEADS, HEAD), cosine, sine))
    keys = low(rotate(key_pre.reshape(length, KV_HEADS, HEAD), cosine, sine))
    values = low_back(low(multiply(normed, w_value) + b_value)).reshape(length, KV_HEADS, HEAD)
    mixed = attention(queries, keys, values, places, docs)
    mixed = low_back(low(mixed))
    hidden_mid = hidden + low_back(multiply(mixed, w_out))
    normed_two = low(hidden_mid * rms_scale(hidden_mid) * gain_ffn)
    gate = low_back(multiply(normed_two, w_gate))
    upper = low_back(multiply(normed_two, w_up))
    inner = low(jax.nn.silu(gate) * upper)
    return hidden_mid + low_back(multiply(inner, w_down))

def reference(tokens, cotangent, doc_ids, block_order, w_query, w_key, w_value, w_out, b_query, b_key, b_value, gain_attn, w_gate, w_up, w_down, gain_ffn):
    params = tuple((item.astype(jnp.float32) for item in (w_query, w_key, w_value, w_out, b_query, b_key, b_value, gain_attn, w_gate, w_up, w_down, gain_ffn)))
    places = stored_places(block_order)
    cosine, sine = rotary_tables(places)

    def forward(inputs, weights):
        return lax.map(lambda item: layer(weights, item[0], item[1], places, cosine, sine), (inputs, doc_ids))
    hidden = tokens.astype(jnp.float32)
    result, pullback = jax.vjp(forward, hidden, params)
    grad_in, grads = pullback(cotangent.astype(jnp.float32))
    return (result.astype(jnp.bfloat16), grad_in.astype(jnp.bfloat16), grads[0], grads[1], grads[2], grads[3], grads[4], grads[5], grads[6], grads[7], grads[8], grads[9], grads[10], grads[11])
```

```python
import jax
import jax.numpy as jnp
from jax import lax
from jax.sharding import PartitionSpec as P

HEAD = 128
PIECES = 4
PIECES_DOWN = 4


THETA = 1000000.0
EPS = 1e-06
MASKED = -1e30


def rotary_tables(places, head):
    half = head // 2
    freqs = THETA ** (-jnp.arange(half, dtype=jnp.float32) / half)
    angles = places.astype(jnp.float32)[:, None] * freqs[None, :]
    return (jnp.cos(angles), jnp.sin(angles))


def rotate(values, cosine, sine):
    half = values.shape[-1] // 2
    front = values[..., :half]
    back_half = values[..., half:]
    cosine = cosine[:, None, :]
    sine = sine[:, None, :]
    return jnp.concatenate(
        [front * cosine - back_half * sine, back_half * cosine + front * sine], axis=-1
    )


def inverse_scale(hidden):
    return lax.rsqrt(jnp.mean(hidden * hidden, axis=-1, keepdims=True) + EPS)


def norm_backward(hidden, scale_rows, gain, grad_normed):
    weighted = grad_normed * gain
    inner_mean = jnp.mean(weighted * hidden, axis=-1, keepdims=True)
    grad_hidden = scale_rows * weighted - hidden * scale_rows * scale_rows * scale_rows * inner_mean
    grad_gain = jnp.sum(grad_normed * hidden * scale_rows, axis=0)
    return (grad_hidden, grad_gain)


def group_scores(query_group, key_group, allowed, scale):
    scores = (
        jnp.einsum("qgd,ld->gql", query_group, key_group, preferred_element_type=jnp.float32)
        * scale
    )
    return jnp.where(allowed[None], scores, MASKED)


def gate_grads(grad_inner, gate, upper):
    sigma = jax.nn.sigmoid(gate)
    grad_gate = (grad_inner * upper * sigma * (1.0 + gate * (1.0 - sigma))).astype(jnp.bfloat16)
    grad_upper = (grad_inner * gate * sigma).astype(jnp.bfloat16)
    return (grad_gate, grad_upper)


def line_sum(piece, axis):
    count = lax.axis_size(axis)
    index = lax.axis_index(axis)
    piece = piece.astype(jnp.bfloat16)
    if count == 1:
        return piece
    if count % 2:
        return lax.psum(piece, axis)
    half = count // 2

    def plus(left, right):
        return (left.astype(jnp.float32) + right.astype(jnp.float32)).astype(jnp.bfloat16)

    for step in range(half - 1):
        pairs = [(step, step + 1), (count - 1 - step, count - 2 - step)]
        piece = plus(piece, lax.ppermute(piece, axis, pairs))
    piece = plus(piece, lax.ppermute(piece, axis, [(half - 1, half), (half, half - 1)]))
    for step in range(half - 1):
        low, high = half - 1 - step, half + step
        moved = lax.ppermute(piece, axis, [(low, low - 1), (high, high + 1)])
        piece = jnp.where((index == low - 1) | (index == high + 1), moved, piece)
    return piece


def summed_rows(product, rows, pieces, axis):
    size = rows // pieces
    parts = [line_sum(product(part * size, size), axis) for part in range(pieces)]
    return jnp.concatenate(parts, axis=0).astype(jnp.float32)


def spread(row, count, depth):
    part = row.reshape(count, -1)
    return jnp.pad(part, ((0, 0), (0, depth - part.shape[1]))).reshape(-1)


def shards(
    tokens,
    cotangent,
    doc_ids,
    block_order,
    w_query,
    w_key,
    w_value,
    w_out,
    b_query,
    b_key,
    b_value,
    gain_attn,
    w_gate,
    w_up,
    w_down,
    gain_ffn,
):
    ctx_count = lax.axis_size("ctx")
    ctx_index = lax.axis_index("ctx")
    rows = tokens.shape[1]
    width = tokens.shape[2]
    block = rows // 2
    head = HEAD
    kv_width = w_key.shape[1]
    kv_heads = kv_width // head
    heads = width // head
    group = heads // kv_heads
    scale = head ** (-0.5)
    blocks = jnp.stack([block_order, 2 * ctx_count - 1 - block_order], axis=1).reshape(-1)
    places = (blocks[:, None] * block + jnp.arange(block, dtype=jnp.int32)[None, :]).reshape(-1)
    own_places = lax.dynamic_slice_in_dim(places, ctx_index * rows, rows)
    key_docs = doc_ids[0]
    own_docs = lax.dynamic_slice_in_dim(key_docs, ctx_index * rows, rows)
    allowed = (places[None, :] <= own_places[:, None]) & (key_docs[None, :] == own_docs[:, None])
    cosine, sine = rotary_tables(own_places, head)
    fsdp_count = lax.axis_size("fsdp")
    depth = w_query.shape[0]
    small = jnp.concatenate([b_query, b_key, b_value, gain_attn, gain_ffn]).reshape(1, -1)
    small_all = lax.all_gather(small, "fsdp", axis=0, tiled=True)
    cuts = [0, b_query.shape[0]]
    for item in (b_key, b_value, gain_attn, gain_ffn):
        cuts.append(cuts[-1] + item.shape[0])
    query_bias, key_bias, value_bias, attn_gain, ffn_gain = (
        small_all[:, cuts[at] : cuts[at + 1]].reshape(-1) for at in range(5)
    )
    kv_all = lax.all_gather(
        jnp.concatenate([w_key, w_value], axis=1), "fsdp", axis=0, tiled=True
    )
    key_all, value_all = kv_all[:, :kv_width], kv_all[:, kv_width:]
    query_all = lax.all_gather(w_query, "fsdp", axis=0, tiled=True)
    grad_out = cotangent[0]
    grad_rows = lax.all_gather(grad_out, "fsdp", axis=0, tiled=True)
    out_all = lax.all_gather(w_out, "fsdp", axis=0, tiled=True)
    attn_gain = attn_gain.astype(jnp.float32)
    ffn_gain = ffn_gain.astype(jnp.float32)
    hidden = tokens[0].astype(jnp.float32)
    scale_one = inverse_scale(hidden)
    normed = (hidden * scale_one * attn_gain).astype(jnp.bfloat16)
    query_pre = jnp.dot(normed, query_all, preferred_element_type=jnp.float32) + query_bias.astype(
        jnp.float32
    )
    key_pre = jnp.dot(normed, key_all, preferred_element_type=jnp.float32) + key_bias.astype(
        jnp.float32
    )
    queries = rotate(query_pre.reshape(rows, heads, head), cosine, sine).astype(jnp.bfloat16)
    keys = (
        rotate(key_pre.reshape(rows, kv_heads, head), cosine, sine)
        .astype(jnp.bfloat16)
        .reshape(rows, kv_width)
    )
    values = (
        jnp.dot(normed, value_all, preferred_element_type=jnp.float32)
        + value_bias.astype(jnp.float32)
    ).astype(jnp.bfloat16)
    every = lax.all_gather(jnp.concatenate([keys, values], axis=1), "ctx", axis=0, tiled=True)
    every_key, every_value = every[:, :kv_width], every[:, kv_width:]
    query_groups = queries.reshape(rows, kv_heads, group, head)
    mixed_parts = []
    log_totals = []
    for index in range(kv_heads):
        key_group = every_key[:, index * head : (index + 1) * head]
        value_group = every_value[:, index * head : (index + 1) * head]
        scores = group_scores(query_groups[:, index], key_group, allowed, scale)
        peak = jnp.max(scores, axis=-1, keepdims=True)
        raised = jnp.exp(scores - peak)
        total = jnp.sum(raised, axis=-1, keepdims=True)
        probs = (raised / total).astype(jnp.bfloat16)
        mixed_parts.append(
            jnp.einsum("gql,ld->qgd", probs, value_group, preferred_element_type=jnp.float32)
        )
        log_totals.append(peak + jnp.log(total))
    mixed = jnp.stack(mixed_parts, axis=1).reshape(rows, width).astype(jnp.bfloat16)
    hidden_mid = hidden + jnp.dot(mixed, out_all, preferred_element_type=jnp.float32)
    scale_two = inverse_scale(hidden_mid)
    normed_two = (hidden_mid * scale_two * ffn_gain).astype(jnp.bfloat16)
    rows_all = lax.all_gather(normed_two, "fsdp", axis=0, tiled=True)
    gate = jnp.dot(rows_all, w_gate, preferred_element_type=jnp.float32)
    upper = jnp.dot(rows_all, w_up, preferred_element_type=jnp.float32)
    inner = (jax.nn.silu(gate) * upper).astype(jnp.bfloat16)
    grad_inner = jnp.einsum("td,fd->tf", grad_rows, w_down, preferred_element_type=jnp.float32)
    grad_gate, grad_upper = gate_grads(grad_inner, gate, upper)
    first_term = jnp.einsum("tf,df->td", grad_gate, w_gate, preferred_element_type=jnp.float32)
    grad_normed_two = lax.psum_scatter(
        (
            first_term + jnp.einsum("tf,df->td", grad_upper, w_up, preferred_element_type=jnp.float32)
        ).astype(jnp.bfloat16),
        "fsdp",
        scatter_dimension=0,
        tiled=True,
    ).astype(jnp.float32)
    mlp_out = lax.psum_scatter(
        jnp.dot(inner, w_down, preferred_element_type=jnp.float32).astype(jnp.bfloat16),
        "fsdp",
        scatter_dimension=0,
        tiled=True,
    )
    output = (hidden_mid + mlp_out.astype(jnp.float32)).astype(jnp.bfloat16)

    def down_rows(start, size):
        return jnp.einsum(
            "tf,td->fd", inner[:, start : start + size], grad_rows, preferred_element_type=jnp.float32
        )

    def gate_rows(start, size):
        return jnp.einsum(
            "td,tf->df", rows_all[:, start : start + size], grad_gate, preferred_element_type=jnp.float32
        )

    def up_rows(start, size):
        return jnp.einsum(
            "td,tf->df", rows_all[:, start : start + size], grad_upper, preferred_element_type=jnp.float32
        )

    grad_down_w = summed_rows(down_rows, inner.shape[1], PIECES_DOWN, "ctx")
    grad_gate_w = summed_rows(gate_rows, width, PIECES, "ctx")
    grad_up_w = summed_rows(up_rows, width, PIECES, "ctx")
    grad_norm_two, grad_gain_ffn = norm_backward(hidden_mid, scale_two, ffn_gain, grad_normed_two)
    grad_mid = grad_out.astype(jnp.float32) + grad_norm_two
    grad_mid_low = grad_mid.astype(jnp.bfloat16)
    grad_mixed = jnp.einsum(
        "te,de->td", grad_mid_low, out_all, preferred_element_type=jnp.float32
    ).astype(jnp.bfloat16)
    grad_mixed_groups = grad_mixed.reshape(rows, kv_heads, group, head)
    grad_query_parts = []
    grad_key_parts = []
    grad_value_parts = []
    for index in range(kv_heads):
        key_group = every_key[:, index * head : (index + 1) * head]
        value_group = every_value[:, index * head : (index + 1) * head]
        query_group = query_groups[:, index]
        grad_group = grad_mixed_groups[:, index]
        scores = group_scores(query_group, key_group, allowed, scale)
        probs = jnp.exp(scores - log_totals[index])
        grad_probs = jnp.einsum(
            "qgd,ld->gql", grad_group, value_group, preferred_element_type=jnp.float32
        )
        grad_value_parts.append(
            jnp.einsum(
                "gql,qgd->ld",
                probs.astype(jnp.bfloat16),
                grad_group,
                preferred_element_type=jnp.float32,
            )
        )
        delta = jnp.sum(probs * grad_probs, axis=-1, keepdims=True)
        grad_scores = (probs * (grad_probs - delta) * scale).astype(jnp.bfloat16)
        grad_query_parts.append(
            jnp.einsum("gql,ld->qgd", grad_scores, key_group, preferred_element_type=jnp.float32)
        )
        grad_key_parts.append(
            jnp.einsum("gql,qgd->ld", grad_scores, query_group, preferred_element_type=jnp.float32)
        )
    grad_every_key = jnp.concatenate(grad_key_parts, axis=1)
    grad_every_value = jnp.concatenate(grad_value_parts, axis=1)
    own_grad = lax.psum_scatter(
        jnp.concatenate([grad_every_key, grad_every_value], axis=1).astype(jnp.bfloat16),
        "ctx",
        scatter_dimension=0,
        tiled=True,
    ).astype(jnp.float32)
    own_grad_key, own_grad_value = own_grad[:, :kv_width], own_grad[:, kv_width:]
    grad_query_pre = (
        rotate(jnp.stack(grad_query_parts, axis=1).reshape(rows, heads, head), cosine, -sine)
        .astype(jnp.bfloat16)
        .reshape(rows, width)
    )
    grad_key_pre = (
        rotate(own_grad_key.reshape(rows, kv_heads, head), cosine, -sine)
        .astype(jnp.bfloat16)
        .reshape(rows, kv_width)
    )
    grad_value_pre = own_grad_value.astype(jnp.bfloat16)
    grad_normed = jnp.einsum(
        "te,de->td", grad_query_pre, query_all, preferred_element_type=jnp.float32
    )
    grad_normed = grad_normed + jnp.einsum(
        "te,de->td", grad_key_pre, key_all, preferred_element_type=jnp.float32
    )
    grad_normed = grad_normed + jnp.einsum(
        "te,de->td", grad_value_pre, value_all, preferred_element_type=jnp.float32
    )
    grad_norm_one, grad_gain_attn = norm_backward(hidden, scale_one, attn_gain, grad_normed)
    grad_tokens = (grad_mid + grad_norm_one).astype(jnp.bfloat16)
    grad_projections = jnp.concatenate([grad_query_pre, grad_key_pre, grad_value_pre], axis=1)
    projection_part = jnp.einsum(
        "tc,te->ce", normed, grad_projections, preferred_element_type=jnp.float32
    )
    output_part = jnp.einsum("tc,te->ce", mixed, grad_mid_low, preferred_element_type=jnp.float32)
    grad_b_query = jnp.sum(grad_query_pre.astype(jnp.float32), axis=0)
    grad_b_key = jnp.sum(grad_key_pre.astype(jnp.float32), axis=0)
    grad_b_value = jnp.sum(grad_value_pre.astype(jnp.float32), axis=0)
    kv_depth = kv_width // fsdp_count
    small_part = jnp.stack(
        [
            grad_gain_attn,
            grad_gain_ffn,
            grad_b_query,
            spread(grad_b_key, fsdp_count, depth),
            spread(grad_b_value, fsdp_count, depth),
        ],
        axis=1,
    )
    small_part = jnp.pad(small_part, ((0, 0), (0, 128 - small_part.shape[1])))
    attn_shard = lax.psum_scatter(
        jnp.concatenate([projection_part, output_part, small_part], axis=1).astype(jnp.bfloat16),
        "fsdp",
        scatter_dimension=0,
        tiled=True,
    )
    attn_shard = line_sum(attn_shard, "ctx").astype(jnp.float32)
    grad_w_query = attn_shard[:, :width]
    grad_w_key = attn_shard[:, width : width + kv_width]
    grad_w_value = attn_shard[:, width + kv_width : width + 2 * kv_width]
    grad_w_out = attn_shard[:, width + 2 * kv_width : 2 * width + 2 * kv_width]
    small_rows = attn_shard[:, 2 * width + 2 * kv_width :]
    return (
        output[None],
        grad_tokens[None],
        grad_w_query,
        grad_w_key,
        grad_w_value,
        grad_w_out,
        small_rows[:, 2],
        small_rows[:kv_depth, 3],
        small_rows[:kv_depth, 4],
        small_rows[:, 0],
        grad_gate_w,
        grad_up_w,
        grad_down_w,
        small_rows[:, 1],
    )


def solution(mesh):
    return jax.shard_map(
        shards,
        mesh=mesh,
        in_specs=(
            P("fsdp", "ctx", None),
            P("fsdp", "ctx", None),
            P("fsdp", None),
            P(),
            P("fsdp", None),
            P("fsdp", None),
            P("fsdp", None),
            P("fsdp", None),
            P("fsdp"),
            P("fsdp"),
            P("fsdp"),
            P("fsdp"),
            P(None, "fsdp"),
            P(None, "fsdp"),
            P("fsdp", None),
            P("fsdp"),
        ),
        out_specs=(
            P("fsdp", "ctx", None),
            P("fsdp", "ctx", None),
            P("fsdp", None),
            P("fsdp", None),
            P("fsdp", None),
            P("fsdp", None),
            P("fsdp"),
            P("fsdp"),
            P("fsdp"),
            P("fsdp"),
            P(None, "fsdp"),
            P(None, "fsdp"),
            P("fsdp", None),
            P("fsdp"),
        ),
        check_vma=False,
    )
```

```python
import functools

import jax
import jax.numpy as jnp
from jax import lax
from jax.experimental import pallas as pl
from jax.experimental.layout import Layout, with_layout_constraint
from jax.experimental.pallas import tpu as pltpu
from jax.sharding import PartitionSpec as P

HEAD = 128
CHUNKS = 5

THETA = 1000000.0
EPS = 1e-06
MASKED = -1e30
BF16 = jnp.bfloat16
F32 = jnp.float32


def dot_nn(left, right):
    return lax.dot_general(left, right, (((1,), (0,)), ((), ())), preferred_element_type=F32)


def dot_nt(left, right):
    return lax.dot_general(left, right, (((1,), (1,)), ((), ())), preferred_element_type=F32)


def cost(flops, *arrays, exps=0):
    moved = sum(item.size * item.dtype.itemsize for item in arrays)
    return pl.CostEstimate(flops=int(flops), bytes_accessed=int(moved), transcendentals=int(exps))


def shape_of(shape, dtype):
    return jax.ShapeDtypeStruct(shape, dtype)


VMEM = pl.BlockSpec(memory_space=pltpu.VMEM)


def room(mib):
    return pltpu.CompilerParams(vmem_limit_bytes=mib << 20)


def whole(shape):
    return pl.BlockSpec(shape, lambda *_: (0,) * len(shape))


def flat(value):
    return with_layout_constraint(value, Layout(major_to_minor=tuple(range(value.ndim))))


def exchange(value, axis, mask):
    count = lax.axis_size(axis)
    return flat(lax.ppermute(flat(value), axis, [(at, at ^ mask) for at in range(count)]))


def shift(value, axis, by):
    count = lax.axis_size(axis)
    return flat(lax.ppermute(flat(value), axis, [(at, (at + by) % count) for at in range(count)]))


def line_sum(piece, axis):
    count = lax.axis_size(axis)
    index = lax.axis_index(axis)
    piece = piece.astype(BF16)
    if count == 1:
        return piece
    if count % 2:
        return lax.psum(piece, axis)
    half = count // 2

    def plus(left, right):
        return (left.astype(F32) + right.astype(F32)).astype(BF16)

    for step in range(half - 1):
        pairs = [(step, step + 1), (count - 1 - step, count - 2 - step)]
        piece = plus(piece, lax.ppermute(piece, axis, pairs))
    piece = plus(piece, lax.ppermute(piece, axis, [(half - 1, half), (half, half - 1)]))
    for step in range(half - 1):
        low, high = half - 1 - step, half + step
        moved = lax.ppermute(piece, axis, [(low, low - 1), (high, high + 1)])
        piece = jnp.where((index == low - 1) | (index == high + 1), moved, piece)
    return piece


def turn(value, cosine, sine):
    return value * cosine + pltpu.roll(value, value.shape[-1] // 2, 1) * sine


def prepare_kernel(count, depth, kv_depth, index_ref, tokens_ref, *refs):
    pieces = refs[:count]
    normed_ref, turned_ref, scale_ref, query_ref, kv_ref, attn_ref, ffn_ref = refs[count:]
    width = query_ref.shape[1]
    tall, lanes = pieces[0].shape
    kv_width = kv_depth * count
    vectors = jnp.zeros((tall, width), F32)
    bias = jnp.zeros((tall, kv_width), F32)
    lane = lax.broadcasted_iota(jnp.int32, (lanes, width), 0)
    column = lax.broadcasted_iota(jnp.int32, (lanes, width), 1)
    lane_kv = lax.broadcasted_iota(jnp.int32, (lanes, kv_width), 0)
    column_kv = lax.broadcasted_iota(jnp.int32, (lanes, kv_width), 1)
    for at in range(count):
        owner = index_ref[0] ^ at
        pick = (column == lane + owner * depth) & (lane < depth)
        vectors = vectors + dot_nn(pieces[at][...], jnp.where(pick, 1.0, 0.0).astype(BF16))
        pick = (column_kv == lane_kv + owner * kv_depth) & (lane_kv < kv_depth)
        bias = bias + dot_nn(pieces[at][...], jnp.where(pick, 1.0, 0.0).astype(BF16))
    query_ref[...] = vectors[0:1, :]
    attn_ref[...] = vectors[3:4, :]
    ffn_ref[...] = vectors[4:5, :]
    kv_ref[:, :kv_width] = bias[1:2, :]
    kv_ref[:, kv_width:] = bias[2:3, :]
    hidden = tokens_ref[...].astype(F32)
    scale = lax.rsqrt(jnp.mean(hidden * hidden, axis=-1, keepdims=True) + EPS)
    normed = hidden * scale * vectors[3:4, :]
    scale_ref[...] = scale
    normed_ref[...] = normed.astype(BF16)
    turned_ref[...] = normed.T.astype(BF16)


def prepare(index, tokens, pieces, depth, kv_depth):
    rows, width = tokens.shape
    count = len(pieces)
    return pl.pallas_call(
        functools.partial(prepare_kernel, count, depth, kv_depth),
        grid_spec=pltpu.PrefetchScalarGridSpec(
            num_scalar_prefetch=1,
            grid=(1,),
            in_specs=[whole((rows, width))] + [whole(item.shape) for item in pieces],
            out_specs=[
                whole((rows, width)),
                whole((width, rows)),
                whole((rows, 1)),
                whole((1, width)),
                whole((1, 2 * kv_depth * count)),
                whole((1, width)),
                whole((1, width)),
            ],
        ),
        out_shape=[
            shape_of((rows, width), BF16),
            shape_of((width, rows), BF16),
            shape_of((rows, 1), F32),
            shape_of((1, width), F32),
            shape_of((1, 2 * kv_depth * count), F32),
            shape_of((1, width), F32),
            shape_of((1, width), F32),
        ],
        compiler_params=room(12),
        name="prepare",
    )(index, tokens, *pieces)


def project_kernel(turned, count, index_ref, normed_ref, *refs):
    pieces = refs[:count]
    bias_ref, cos_ref, sin_ref, out_ref, weight_ref = refs[count:]
    depth = pieces[0].shape[0]
    for at in range(count):
        start = pl.multiple_of((index_ref[0] ^ at) * depth, 16)
        weight_ref[pl.ds(start, depth), :] = pieces[at][...]
    raw = dot_nn(normed_ref[...], weight_ref[...]) + bias_ref[...]
    for at in range(raw.shape[1] // HEAD):
        part = raw[:, at * HEAD : (at + 1) * HEAD]
        if at < turned:
            part = turn(part, cos_ref[...], sin_ref[...])
        out_ref[:, at * HEAD : (at + 1) * HEAD] = part.astype(BF16)


def project(normed, pieces, index, bias, cosine, sine, first, columns, tile, turned):
    rows, width = normed.shape
    count = len(pieces)
    depth = pieces[0].shape[0]
    offset = first // tile
    return pl.pallas_call(
        functools.partial(project_kernel, turned, count),
        grid_spec=pltpu.PrefetchScalarGridSpec(
            num_scalar_prefetch=1,
            grid=(columns // tile,),
            in_specs=[whole((rows, width))]
            + [pl.BlockSpec((depth, tile), lambda at, index: (0, at + offset))] * count
            + [
                pl.BlockSpec((1, tile), lambda at, index: (0, at)),
                whole(cosine.shape),
                whole(sine.shape),
            ],
            out_specs=[
                pl.BlockSpec((rows, tile), lambda at, index: (0, at)),
                pl.BlockSpec((width, tile), lambda at, index: (0, at)),
            ],
        ),
        out_shape=[shape_of((rows, columns), BF16), shape_of((width, columns), BF16)],
        cost_estimate=pl.CostEstimate(
            flops=2 * rows * width * columns, bytes_accessed=4 * width * columns, transcendentals=0
        ),
        compiler_params=room(20),
        name="project",
    )(index, normed, *pieces, bias, cosine, sine)


def outer_rel_kernel(count, parts, index_ref, *refs):
    left_ref = refs[0]
    rights, extra, outs = refs[1 : 1 + parts], refs[1 + parts : -count], refs[-count:]
    depth = outs[0].shape[0]
    for which in range(count):
        rows = pl.ds(pl.multiple_of((index_ref[0] ^ which) * depth, 16), depth)
        left = left_ref[rows, :]
        start = 0
        for right in rights:
            outs[which][:, start : start + right.shape[1]] = dot_nn(left, right[...]).astype(BF16)
            start += right.shape[1]
        for item in extra:
            outs[which][:, start : start + item.shape[1]] = item[rows, :]
            start += item.shape[1]


def outer_rel(left, rights, extra, index, count):
    width, rows = left.shape
    depth = width // count
    columns = sum(item.shape[1] for item in rights) + sum(item.shape[1] for item in extra)
    return pl.pallas_call(
        functools.partial(outer_rel_kernel, count, len(rights)),
        in_specs=[pl.BlockSpec(memory_space=pltpu.SMEM)] + [VMEM] * (1 + len(rights) + len(extra)),
        out_specs=[VMEM] * count,
        out_shape=[shape_of((depth, columns), BF16)] * count,
        compiler_params=room(16),
        cost_estimate=pl.CostEstimate(
            flops=2 * width * rows * columns, bytes_accessed=2 * width * columns, transcendentals=0
        ),
        name="outer_rel",
    )(index, left, *rights, *extra)


def join_kernel(mixed_ref, weight_ref, tokens_ref, gain_ref, mid_ref, normed_ref, scale_ref):
    hidden = tokens_ref[...].astype(F32) + dot_nn(mixed_ref[...], weight_ref[...])
    mid_ref[...] = hidden
    scale = lax.rsqrt(jnp.mean(hidden * hidden, axis=-1, keepdims=True) + EPS)
    scale_ref[...] = scale
    normed_ref[...] = (hidden * scale * gain_ref[...]).astype(BF16)


def join(mixed, weight, tokens, gain):
    rows, width = mixed.shape
    return pl.pallas_call(
        join_kernel,
        in_specs=[VMEM] * 4,
        out_specs=[VMEM] * 3,
        out_shape=[shape_of((rows, width), F32), shape_of((rows, width), BF16), shape_of((rows, 1), F32)],
        compiler_params=room(12),
        cost_estimate=pl.CostEstimate(
            flops=2 * rows * width * width, bytes_accessed=2 * width * width, transcendentals=0
        ),
        name="join",
    )(mixed, weight, tokens, gain)


def part_kernel(count, *refs):
    terms = refs[:count]
    mid_ref, scale_ref, gain_ref, grad_ref, weight_ref = refs[count : count + 5]
    gm_ref, low_ref, gain_out, mixed_ref = refs[count + 5 :]
    total = terms[0][...].astype(F32)
    for item in terms[1:]:
        total = total + item[...].astype(F32)
    total = total.T
    hidden = mid_ref[...]
    scale = scale_ref[...]
    weighted = total * gain_ref[...]
    inner_mean = jnp.mean(weighted * hidden, axis=-1, keepdims=True)
    gain_out[...] = jnp.sum(total * (hidden * scale), axis=0, keepdims=True)
    grad = grad_ref[...].astype(F32) + scale * weighted - hidden * (scale * scale * scale * inner_mean)
    gm_ref[...] = grad
    low = grad.astype(BF16)
    low_ref[...] = low
    mixed_ref[...] = dot_nt(low, weight_ref[...]).astype(BF16)


def part(terms, hidden_mid, scale, gain, grad_out, weight):
    rows, width = hidden_mid.shape
    return pl.pallas_call(
        functools.partial(part_kernel, len(terms)),
        in_specs=[VMEM] * (len(terms) + 5),
        out_specs=[VMEM] * 4,
        out_shape=[
            shape_of((rows, width), F32),
            shape_of((rows, width), BF16),
            shape_of((1, width), F32),
            shape_of((rows, width), BF16),
        ],
        compiler_params=room(16),
        cost_estimate=pl.CostEstimate(
            flops=2 * rows * width * width, bytes_accessed=2 * width * width + 20 * rows * width, transcendentals=0
        ),
        name="part",
    )(*terms, hidden_mid, scale, gain, grad_out, weight)


def fill_mask(bias_ref, key_places, key_docs, row_places, row_docs):
    allowed = (key_places[...] <= row_places[...]) & (key_docs[...] == row_docs[...])
    bias_ref[...] = jnp.where(allowed, 0.0, MASKED)


def attend_kernel(
    group, scale, q_ref, k_ref, v_ref, kp_ref, kd_ref, rp_ref, rd_ref, out_ref, turned_ref, lse_ref, bias_ref
):
    @pl.when(pl.program_id(0) == 0)
    def _():
        fill_mask(bias_ref, kp_ref, kd_ref, rp_ref, rd_ref)

    key = k_ref[...]
    value_t = v_ref[...].T
    for at in range(group):
        query = q_ref[:, at * HEAD : (at + 1) * HEAD]
        scores = dot_nt(key, query) * scale + bias_ref[...]
        peak = jnp.max(scores, axis=0, keepdims=True)
        raised = jnp.exp(scores - peak)
        total = jnp.sum(raised, axis=0, keepdims=True)
        mixed = dot_nn(value_t, raised.astype(BF16)) / total
        turned_ref[at * HEAD : (at + 1) * HEAD, :] = mixed.astype(BF16)
        out_ref[:, at * HEAD : (at + 1) * HEAD] = mixed.T.astype(BF16)
        lse_ref[0, at : at + 1, :] = peak + jnp.log(total)


def attend(queries, every, marks, kv_heads):
    rows, width = queries.shape
    length = every.shape[0]
    wide = width // kv_heads
    group = wide // HEAD
    return pl.pallas_call(
        functools.partial(attend_kernel, group, HEAD ** (-0.5)),
        grid=(kv_heads,),
        in_specs=[
            pl.BlockSpec((rows, wide), lambda at: (0, at)),
            pl.BlockSpec((length, HEAD), lambda at: (0, at)),
            pl.BlockSpec((length, HEAD), lambda at: (0, at + kv_heads)),
        ]
        + [whole(item.shape) for item in marks],
        out_specs=[
            pl.BlockSpec((rows, wide), lambda at: (0, at)),
            pl.BlockSpec((wide, rows), lambda at: (at, 0)),
            pl.BlockSpec((1, group, rows), lambda at: (at, 0, 0)),
        ],
        out_shape=[
            shape_of((rows, width), BF16),
            shape_of((width, rows), BF16),
            shape_of((kv_heads, group, rows), F32),
        ],
        scratch_shapes=[pltpu.VMEM((length, rows), F32)],
        cost_estimate=pl.CostEstimate(
            flops=4 * rows * length * width * 4,
            bytes_accessed=4 * rows * width + 2 * every.size,
            transcendentals=rows * length * width // HEAD,
        ),
        compiler_params=room(24),
        name="attend",
    )(queries, every, every, *marks)


def attend_back_kernel(
    group,
    scale,
    q_ref,
    k_ref,
    v_ref,
    lse_ref,
    grad_ref,
    cos_ref,
    sin_ref,
    kp_ref,
    kd_ref,
    rp_ref,
    rd_ref,
    gq_ref,
    gk_ref,
    gv_ref,
    bias_ref,
):
    @pl.when(pl.program_id(0) == 0)
    def _():
        fill_mask(bias_ref, kp_ref, kd_ref, rp_ref, rd_ref)

    key = k_ref[...]
    value = v_ref[...]
    key_t = key.T
    grad_key = None
    grad_value = None
    for at in range(group):
        part = slice(at * HEAD, (at + 1) * HEAD)
        query = q_ref[:, part]
        grad = grad_ref[:, part]
        scores = dot_nt(key, query) * scale + bias_ref[...]
        probs = jnp.exp(scores - lse_ref[0, at : at + 1, :])
        grad_probs = dot_nt(value, grad)
        delta = jnp.sum(probs * grad_probs, axis=0, keepdims=True)
        grad_scores = (probs * (grad_probs - delta) * scale).astype(BF16)
        value_term = dot_nn(probs.astype(BF16), grad)
        key_term = dot_nn(grad_scores, query)
        grad_value = value_term if grad_value is None else grad_value + value_term
        grad_key = key_term if grad_key is None else grad_key + key_term
        grad_query = dot_nn(key_t, grad_scores).T
        gq_ref[:, part] = turn(grad_query, cos_ref[...], sin_ref[...]).astype(BF16)
    gk_ref[...] = grad_key.astype(BF16)
    gv_ref[...] = grad_value.astype(BF16)


def attend_back(queries, every, lse, grad_mixed, cosine, sine, marks, kv_heads):
    rows, width = queries.shape
    length = every.shape[0]
    wide = width // kv_heads
    group = wide // HEAD
    by_group = pl.BlockSpec((rows, wide), lambda at: (0, at))
    by_head = pl.BlockSpec((length, HEAD), lambda at: (0, at))
    return pl.pallas_call(
        functools.partial(attend_back_kernel, group, HEAD ** (-0.5)),
        grid=(kv_heads,),
        in_specs=[
            by_group,
            by_head,
            pl.BlockSpec((length, HEAD), lambda at: (0, at + kv_heads)),
            pl.BlockSpec((1, group, rows), lambda at: (at, 0, 0)),
            by_group,
            whole(cosine.shape),
            whole(sine.shape),
        ]
        + [whole(item.shape) for item in marks],
        out_specs=[by_group, by_head, by_head],
        out_shape=[
            shape_of((rows, width), BF16),
            shape_of((length, kv_heads * HEAD), BF16),
            shape_of((length, kv_heads * HEAD), BF16),
        ],
        scratch_shapes=[pltpu.VMEM((length, rows), F32)],
        cost_estimate=pl.CostEstimate(
            flops=10 * rows * length * width * 3,
            bytes_accessed=8 * rows * width + 4 * every.size,
            transcendentals=rows * length * width // HEAD,
        ),
        compiler_params=room(32),
        name="attend_back",
    )(queries, every, every, lse, grad_mixed, cosine, sine, *marks)


def flip_kernel(*refs):
    count = len(refs) // 2
    for at in range(count):
        refs[count + at][...] = refs[at][...].T


def flip(*arrays):
    deep, wide = arrays[0].shape
    tile = 256
    return pl.pallas_call(
        flip_kernel,
        grid=(wide // tile,),
        in_specs=[pl.BlockSpec((deep, tile), lambda at: (0, at))] * len(arrays),
        out_specs=[pl.BlockSpec((tile, deep), lambda at: (at, 0))] * len(arrays),
        out_shape=[shape_of((wide, deep), item.dtype) for item in arrays],
        cost_estimate=pl.CostEstimate(flops=0, bytes_accessed=4 * len(arrays) * deep * wide, transcendentals=0),
        compiler_params=room(20),
        name="flip",
    )(*arrays)


def feed_kernel(slot, *refs):
    x_ref, c_ref, gate_ref, up_ref, down_ref = refs[:5]
    inner_ref, gg_ref, gu_ref = refs[-3:]
    rows = x_ref.shape[0]
    units = gate_ref.shape[0]
    part = slice(slot * rows, (slot + 1) * rows)
    step = units // 2
    for start in range(0, units, step):
        unit = slice(start, start + step)
        gate = dot_nt(gate_ref[unit, :], x_ref[...])
        upper = dot_nt(up_ref[unit, :], x_ref[...])
        grad = dot_nt(down_ref[unit, :], c_ref[...])
        half = 0.5 * jnp.tanh(0.5 * gate)
        sigma = half + 0.5
        smooth = gate * sigma
        inner_ref[unit, part] = (smooth * upper).astype(BF16)
        gu_ref[unit, part] = (grad * smooth).astype(BF16)
        gg_ref[unit, part] = (grad * upper * (sigma + smooth * (0.5 - half))).astype(BF16)


def feed(x, c, gate_t, up_t, w_down, slot, slots, held):
    rows, width = x.shape
    units = gate_t.shape[0]
    extra = [] if held is None else list(held)
    return pl.pallas_call(
        functools.partial(feed_kernel, slot),
        in_specs=[VMEM] * (5 + len(extra)),
        out_specs=[VMEM] * 3,
        out_shape=[shape_of((units, slots * rows), BF16)] * 3,
        input_output_aliases={5 + at: at for at in range(len(extra))},
        compiler_params=room(12),
        cost_estimate=pl.CostEstimate(
            flops=6 * rows * width * units,
            bytes_accessed=4 * rows * width + 6 * rows * units,
            transcendentals=rows * units,
        ),
        name="feed",
    )(x, c, gate_t, up_t, w_down, *extra)


def back_kernel(count, slot, *refs):
    weights, grads, outs = refs[:count], refs[count : 2 * count], refs[2 * count :]
    width = weights[0].shape[0]
    rows = outs[0].shape[1]
    block = len(outs) * rows
    tile = width // 2
    for start in range(0, width, tile):
        part = slice(start, start + tile)
        total = None
        for weight, grad in zip(weights, grads):
            term = dot_nn(weight[part, :], grad[:, slot * block : (slot + 1) * block])
            total = term if total is None else total + term
        for at, out in enumerate(outs):
            out[part, :] = total[:, at * rows : (at + 1) * rows].astype(BF16)


def back(weights, grads, slot, pieces, rows):
    count = len(weights)
    width, units = weights[0].shape
    return pl.pallas_call(
        functools.partial(back_kernel, count, slot),
        in_specs=[VMEM] * (2 * count),
        out_specs=[VMEM] * pieces,
        out_shape=[shape_of((width, rows), BF16)] * pieces,
        compiler_params=room(12),
        cost_estimate=pl.CostEstimate(
            flops=2 * count * pieces * rows * width * units,
            bytes_accessed=2 * count * (width + pieces * rows) * units,
            transcendentals=0,
        ),
        name="back",
    )(*weights, *grads)


def outer_kernel(pieces, left_ref, *refs):
    outs = refs[pieces:]
    size, width = outs[0].shape
    tile = 512
    for start in range(0, width, tile):
        part = slice(start, start + tile)
        right = jnp.concatenate([item[:, part] for item in refs[:pieces]], axis=0)
        total = dot_nn(left_ref[...], right)
        for at, out in enumerate(outs):
            out[:, part] = total[at * size : (at + 1) * size, :].astype(BF16)


def outer(left, right_parts, chunks):
    units, tokens = left.shape
    width = right_parts[0].shape[1]
    pieces = len(right_parts)
    size = units // chunks
    return pl.pallas_call(
        functools.partial(outer_kernel, pieces),
        in_specs=[VMEM] * (1 + pieces),
        out_specs=[VMEM] * chunks,
        out_shape=[shape_of((size, width), BF16)] * chunks,
        compiler_params=room(12),
        cost_estimate=pl.CostEstimate(
            flops=2 * units * tokens * width,
            bytes_accessed=2 * (units * tokens + tokens * width + units * width),
            transcendentals=0,
        ),
        name="outer",
    )(left, *right_parts)


def settle_kernel(count, end_ref, *refs):
    got, sent, out_ref = refs[:count], refs[count : 2 * count], refs[-1]
    size = got[0].shape[0]

    @pl.when(end_ref[0] == 1)
    def _():
        for at in range(count):
            out_ref[at * size : (at + 1) * size, :] = got[at][...].astype(F32)

    @pl.when(end_ref[0] == 0)
    def _():
        for at in range(count):
            out_ref[at * size : (at + 1) * size, :] = sent[at][...].astype(F32)


def settle(is_end, pairs, first, total, held):
    count = len(pairs)
    size, width = pairs[0][0].shape
    tile = 256
    block = pl.BlockSpec((size, tile), lambda at, end: (0, at))
    extra = [] if held is None else [held]
    return pl.pallas_call(
        functools.partial(settle_kernel, count),
        grid_spec=pltpu.PrefetchScalarGridSpec(
            num_scalar_prefetch=1,
            grid=(width // tile,),
            in_specs=[block] * (2 * count) + [pl.BlockSpec(memory_space=pl.ANY)] * len(extra),
            out_specs=pl.BlockSpec((count * size, tile), lambda at, end: (first // count, at)),
        ),
        out_shape=shape_of((total * size, width), F32),
        input_output_aliases={1 + 2 * count: 0} if extra else {},
        compiler_params=room(16),
        cost_estimate=pl.CostEstimate(flops=0, bytes_accessed=8 * count * size * width, transcendentals=0),
        name="settle",
    )(is_end.astype(jnp.int32).reshape(1), *[item[0] for item in pairs], *[item[1] for item in pairs], *extra)


def tie(values, *others):
    return lax.optimization_barrier((values, others))[0]


class Line:
    LAG = 3

    def __init__(self, axis):
        self.axis = axis
        index = lax.axis_index(axis)
        self.is_end = (index == 0) | (index == lax.axis_size(axis) - 1)
        self.simple = lax.axis_size(axis) != 4
        self.chunks, self.mine, self.theirs, self.pairs = [], {}, {}, {}
        self.moving = {}
        self.closed = False
        self.started = self.taken = 0

    def outward(self, token):
        at, old = self.started, self.started - self.LAG
        if self.simple or (at >= len(self.chunks) and not (self.closed and old < len(self.chunks))):
            return token
        if old < 0:
            value = self.chunks[at]
        else:
            theirs = tie(self.theirs[old], token)
            value = (self.mine[old].astype(F32) + theirs.astype(F32)).astype(BF16)
            if at < len(self.chunks):
                value = jnp.where(self.is_end, self.chunks[at], value)
        moved = flat(lax.ppermute(flat(value), self.axis, [(0, 1), (1, 0), (2, 3), (3, 2)]))
        self.moving[at] = (value, moved)
        self.started += 1
        return value

    def inward(self, token):
        if self.simple or self.taken >= self.started:
            return token
        at = self.taken
        value, got = self.moving.pop(at)
        got = tie(got, token)
        if at >= self.LAG:
            self.pairs[at - self.LAG] = (got, value)
        self.taken += 1
        if at >= len(self.chunks):
            return got
        mine = (self.chunks[at].astype(F32) + got.astype(F32)).astype(BF16)
        self.mine[at] = mine
        self.theirs[at] = self.swap(mine)
        return mine

    def swap(self, value):
        wide = lax.axis_size("fsdp")
        pairs = []
        for at, other in enumerate((None, 2, 1, None)):
            for near in range(wide):
                to = at * wide + (near ^ 1) if other is None else other * wide + near
                pairs.append((at * wide + near, to))
        return flat(lax.ppermute(flat(value), (self.axis, "fsdp"), pairs))


class Flow:
    def __init__(self, axis):
        self.token = None
        self.line = Line(axis)

    def enter(self, values):
        return values if self.token is None else tie(values, self.token)

    def leave(self, token):
        self.token = token

    def out(self):
        self.token = self.line.outward(self.token)

    def take(self):
        self.token = self.line.inward(self.token)

    def both(self):
        self.out()
        self.take()

    def add(self, chunks):
        self.line.chunks.extend(chunks)

    def drain(self):
        line = self.line
        line.closed = True
        if line.simple:
            sums = [line_sum(chunk, line.axis) for chunk in line.chunks]
            line.pairs = {at: (value, value) for at, value in enumerate(sums)}
            return
        while line.started < len(line.chunks) + line.LAG:
            self.both()
        while line.taken < line.started:
            self.take()

    def settled(self, first, count, held=None, start=0, stop=None):
        pairs = [self.line.pairs[first + at] for at in range(start, stop or count)]
        return settle(self.line.is_end, pairs, start, count, held)


def rotary_tables(places, head):
    half = head // 2
    freqs = THETA ** (-jnp.arange(half, dtype=jnp.float32) / half)
    angles = places.astype(jnp.float32)[:, None] * freqs[None, :]
    cosine, sine = jnp.cos(angles), jnp.sin(angles)
    return jnp.concatenate([cosine, cosine], axis=1), jnp.concatenate([-sine, sine], axis=1)


def inverse_scale(hidden):
    return lax.rsqrt(jnp.mean(hidden * hidden, axis=-1, keepdims=True) + EPS)


def norm_backward(hidden, scale_rows, gain, grad_normed):
    weighted = grad_normed * gain
    inner_mean = jnp.mean(weighted * hidden, axis=-1, keepdims=True)
    grad_hidden = scale_rows * weighted - hidden * scale_rows * scale_rows * scale_rows * inner_mean
    grad_gain = jnp.sum(grad_normed * hidden * scale_rows, axis=0)
    return (grad_hidden, grad_gain)


def turn_rows(value, cosine, sine):
    rows = value.shape[0]
    heads = value.reshape(rows, -1, HEAD)
    half = HEAD // 2
    swapped = jnp.concatenate([heads[..., half:], heads[..., :half]], axis=-1)
    return (heads * cosine[:, None, :] + swapped * sine[:, None, :]).reshape(value.shape)


def shards(
    tokens,
    cotangent,
    doc_ids,
    block_order,
    w_query,
    w_key,
    w_value,
    w_out,
    b_query,
    b_key,
    b_value,
    gain_attn,
    w_gate,
    w_up,
    w_down,
    gain_ffn,
):
    ctx_count = lax.axis_size("ctx")
    ctx_index = lax.axis_index("ctx")
    fsdp_count = lax.axis_size("fsdp")
    rows = tokens.shape[1]
    width = tokens.shape[2]
    depth = w_query.shape[0]
    block = rows // 2
    kv_width = w_key.shape[1]
    kv_heads = kv_width // HEAD

    grad_out = cotangent[0]
    half = rows // 2
    fsdp_index = lax.axis_index("fsdp")
    index = fsdp_index.astype(jnp.int32).reshape(1)

    evens = list(range(2, fsdp_count, 2))
    slots = [(0, 1)]
    for at in range(0, len(evens), 2):
        near = evens[at : at + 2]
        if len(near) == 2:
            slots.append(tuple(near))
            slots.append(tuple(mask ^ 1 for mask in near))
        else:
            slots.append((near[0], near[0] ^ 1))
    order = [mask for pair in slots for mask in pair]

    def far(value, mask, got):
        if mask == 6 and fsdp_count == 8:
            cut = value.shape[0] // 2
            return jnp.concatenate(
                [exchange(got[2][:cut], "fsdp", 4), exchange(got[4][cut:], "fsdp", 2)], axis=0
            )
        return exchange(value, "fsdp", mask)

    w_near = jnp.concatenate([w_key, w_value, w_query], axis=1)
    w_of = {0: w_near}
    for mask in evens[:2]:
        w_of[mask] = exchange(w_near, "fsdp", mask)
    kv_small = kv_width // fsdp_count
    vectors = [b_query, b_key, b_value, gain_attn, gain_ffn]
    lanes = -(-depth // HEAD) * HEAD
    vectors = tie(vectors, w_near)
    small = jnp.stack([jnp.pad(item, (0, lanes - item.shape[0])) for item in vectors], axis=0)
    small = jnp.pad(small, ((0, 16 - len(vectors)), (0, 0)))
    small_of = {mask: exchange(small, "fsdp", mask) if mask else small for mask in [0] + evens}
    for mask in [0] + evens:
        small_of[mask ^ 1] = exchange(small_of[mask], "fsdp", 1)
    small_parts = [small_of[mask] for mask in range(fsdp_count)]

    blocks = jnp.stack([block_order, 2 * ctx_count - 1 - block_order], axis=1).reshape(-1)
    places = (blocks[:, None] * block + jnp.arange(block, dtype=jnp.int32)[None, :]).reshape(-1)
    own_places = lax.dynamic_slice_in_dim(places, ctx_index * rows, rows)
    key_docs = doc_ids[0]
    own_docs = lax.dynamic_slice_in_dim(key_docs, ctx_index * rows, rows)
    marks = (places[:, None], key_docs[:, None], own_places[None, :], own_docs[None, :])
    cosine, sine = rotary_tables(own_places, HEAD)

    tokens_low = tokens[0]
    hidden = tokens_low.astype(F32)
    gate_t, up_t = w_gate.T, w_up.T
    gate_r, up_r, down_r = flip(gate_t, up_t, tie(w_down, cosine, marks))
    normed, normed_t, scale_one, query_bias, kv_bias, attn_gain, ffn_gain = prepare(
        index, tie(tokens_low, gate_r), small_parts, depth, kv_small
    )
    got = tie([w_of[mask] for mask in evens[:2]], normed, kv_bias)
    for mask, value in zip(evens[:2], got):
        w_of[mask] = value
    for mask in evens[2:]:
        w_of[mask] = far(w_near, mask, w_of)
    for mask in [0] + evens:
        w_of[mask ^ 1] = exchange(w_of[mask], "fsdp", 1)
    out_all = lax.all_gather(tie(w_out, got), "fsdp", axis=0, tiled=True)
    w_parts = [w_of[mask] for mask in range(fsdp_count)]

    keys_values, w_kv_all = project(
        normed, w_parts, index, kv_bias, cosine, sine, 0, 2 * kv_width, 2 * kv_width, kv_heads
    )
    every = jnp.zeros((ctx_count, rows, 2 * kv_width), BF16)
    for by in range(ctx_count):
        moved = shift(keys_values, "ctx", by) if by else keys_values
        origin = (ctx_index - by) % ctx_count
        every = lax.dynamic_update_slice(every, moved[None], (origin, 0, 0))
    every = every.reshape(ctx_count * rows, 2 * kv_width)

    c_near = tie(grad_out, keys_values)
    c_of = {0: grad_out}
    for mask in evens[:2]:
        c_of[mask] = exchange(c_near, "fsdp", mask)
    queries, w_q_all = project(
        normed, w_parts, index, query_bias, cosine, sine, 2 * kv_width, width, 2 * HEAD, 2
    )
    got = tie([c_of[mask] for mask in evens[:2]], every, queries)
    for mask, value in zip(evens[:2], got):
        c_of[mask] = value
    for mask in evens[2:]:
        c_of[mask] = far(c_near, mask, c_of)
    queries = tie(queries, got)
    mixed, mixed_t, lse = attend(queries, every, marks, kv_heads)
    got = tie([c_of[mask] for mask in evens[2:]], mixed)
    for mask, value in zip(evens[2:], got):
        c_of[mask] = value
    for mask in [0] + evens:
        c_of[mask ^ 1] = exchange(c_of[mask], "fsdp", 1)
    hidden_mid, normed_two, scale_two = join(mixed, out_all, tokens_low, ffn_gain)

    x_of = {0: normed_two, 1: exchange(normed_two, "fsdp", 1)}
    for mask in evens[:2]:
        x_of[mask] = exchange(normed_two, "fsdp", mask)
    held = None
    for slot, mask in enumerate(order):
        if slot == 2:
            got = tie([x_of[mask] for mask in evens[:2]], held[0])
            for other, value in zip(evens[:2], got):
                x_of[other] = value
            for other in evens[2:]:
                x_of[other] = far(normed_two, other, x_of)
            for other in evens[:2]:
                x_of[other ^ 1] = exchange(x_of[other], "fsdp", 1)
        if slot == 5:
            got = tie([x_of[other] for other in evens[2:]], held[0])
            for other, value in zip(evens[2:], got):
                x_of[other] = value
                x_of[other ^ 1] = exchange(value, "fsdp", 1)
        held = feed(x_of[mask], c_of[mask], gate_t, up_t, w_down, slot, len(order), held)
    inner, grad_gate, grad_upper = held
    x_parts = [x_of[mask] for mask in order]
    c_parts = [c_of[mask] for mask in order]

    flow = Flow("ctx")

    def grads_back(slot):
        gg, gu = flow.enter((grad_gate, grad_upper))
        parts = back([gate_r, up_r], [gg, gu], slot, 2, rows)
        flow.leave(parts[0])
        return dict(zip(slots[slot], parts))

    def rows_down(slot):
        parts = back([down_r], [flow.enter(inner)], slot, 2, rows)
        flow.leave(parts[0])
        return dict(zip(slots[slot], parts))

    def pair_up(terms, mask):
        return terms[mask], exchange(terms[mask ^ 1], "fsdp", 1)

    def pairs_of(terms, pairs):
        for mask in [0] + evens:
            if mask in terms and mask ^ 1 in terms and mask not in pairs:
                pairs[mask] = pair_up(terms, mask)

    def pair_sum(pair):
        return pair[0].astype(F32) + pair[1].astype(F32)

    def far_sums(pairs):
        masks = sorted((mask for mask in pairs if mask), reverse=True)
        near = flow.enter([pairs[mask] for mask in masks])
        sums = [pair_sum(pair).astype(BF16) for pair in near]
        flow.leave(sums[-1])
        return [exchange(value, "fsdp", mask) for mask, value in zip(masks, sums)]

    def gather_up(own, moved):
        total = pair_sum(own)
        for value in moved:
            total = total + value.astype(F32)
        return total

    down_chunks = outer(inner, c_parts, CHUNKS)
    flow.leave(down_chunks[0])
    flow.add(down_chunks)
    terms, pairs = {}, {}
    flow.out()
    for slot in range(len(slots) - 1, 0, -1):
        terms.update(grads_back(slot))
        pairs_of(terms, pairs)
        if slot == len(slots) - 1:
            flow.out()
    flow.take()
    moved = far_sums(pairs)
    flow.out()
    terms.update(grads_back(0))
    pairs_of(terms, pairs)
    flow.take()
    up_chunks = outer(flow.enter(grad_upper), x_parts, CHUNKS)
    flow.leave(up_chunks[0])
    flow.add(up_chunks)
    flow.both()
    gate_chunks = outer(flow.enter(grad_gate), x_parts, CHUNKS)
    flow.leave(gate_chunks[0])
    flow.add(gate_chunks)
    flow.both()
    out_terms, out_pairs = {}, {}
    for slot in range(len(slots) - 1, -1, -1):
        out_terms.update(rows_down(slot))
        pairs_of(out_terms, out_pairs)
    flow.both()
    own_pair, moved = flow.enter((pairs[0], moved))
    grad_mid, grad_mid_low, grad_gain_ffn, grad_mixed = part(
        [*own_pair, *moved], hidden_mid, scale_two, ffn_gain, grad_out, out_all
    )
    flow.leave(grad_mixed)
    flow.out()
    out_moved = far_sums(out_pairs)
    flow.take()
    grad_query_pre, grad_keys, grad_values = attend_back(
        queries, every, lse, flow.enter(grad_mixed), cosine, -sine, marks, kv_heads
    )
    flow.leave(grad_query_pre)
    flow.out()
    grad_keys, grad_values = flow.enter((grad_keys, grad_values))
    own_parts = []
    for by in range(ctx_count):
        start = ((ctx_index + by) % ctx_count) * rows
        piece = jnp.concatenate(
            [
                lax.dynamic_slice_in_dim(grad_keys, start, rows),
                lax.dynamic_slice_in_dim(grad_values, start, rows),
            ],
            axis=1,
        )
        own_parts.append(shift(piece, "ctx", by) if by else piece)
    flow.leave(own_parts[0])
    flow.take()
    out_pieces = outer_rel(mixed_t, [flow.enter(grad_mid_low)], [], index, fsdp_count)
    flow.leave(out_pieces[0])
    attn_out_pairs = {}
    pairs_of(dict(enumerate(out_pieces)), attn_out_pairs)
    flow.both()
    own_out, out_moved = flow.enter((out_pairs[0], out_moved))
    output = (hidden_mid + gather_up(own_out, out_moved).T).astype(BF16)
    flow.leave(output)
    attn_out_moved = far_sums(attn_out_pairs)
    flow.both()
    own_parts = flow.enter(own_parts)
    own_grad = None
    for piece in own_parts:
        own_grad = piece.astype(F32) if own_grad is None else own_grad + piece.astype(F32)
    grad_key_pre = turn_rows(own_grad[:, :kv_width], cosine, -sine).astype(BF16)
    grad_value_pre = own_grad[:, kv_width:].astype(BF16)
    grad_kv_pre = jnp.concatenate([grad_key_pre, grad_value_pre], axis=1)
    attn_pieces = outer_rel(normed_t, [grad_kv_pre, grad_query_pre], [], index, fsdp_count)
    flow.leave(attn_pieces[0])
    attn_pairs = {}
    pairs_of(dict(enumerate(attn_pieces)), attn_pairs)
    flow.both()
    attn_moved = far_sums(attn_pairs)
    flow.both()
    grad_kv_pre = flow.enter(grad_kv_pre)
    grad_normed = jnp.einsum("te,de->td", grad_kv_pre, w_kv_all, preferred_element_type=F32)
    grad_normed = grad_normed + jnp.einsum(
        "te,de->td", grad_query_pre, w_q_all, preferred_element_type=F32
    )
    grad_norm_one, grad_gain_attn = norm_backward(hidden, scale_one, attn_gain, grad_normed)
    grad_tokens = (grad_mid + grad_norm_one).astype(BF16)
    grad_bias = jnp.sum(grad_kv_pre.astype(F32), axis=0)
    small_sums = jnp.stack(
        [
            grad_gain_attn,
            grad_gain_ffn.reshape(-1),
            jnp.sum(grad_query_pre.astype(F32), axis=0),
            jnp.pad(grad_bias, (0, width - 2 * kv_width)),
        ],
        axis=0,
    )
    small_sums = jnp.pad(small_sums, ((0, 4), (0, 0)))
    flow.leave(grad_tokens)
    small_sums = lax.psum(small_sums, ("ctx", "fsdp"))
    flow.both()
    grad_down_w = flow.settled(0, CHUNKS) if not flow.line.simple else None
    if grad_down_w is not None:
        flow.leave(grad_down_w)
    flow.both()
    attn_own, attn_moved, out_own, attn_out_moved = flow.enter(
        (attn_pairs[0], attn_moved, attn_out_pairs[0], attn_out_moved)
    )
    attn_total = gather_up(attn_own, attn_moved).astype(BF16)
    out_total = gather_up(out_own, attn_out_moved).astype(BF16)
    third = depth // 3
    near_kv = jnp.concatenate(
        [attn_total[at * third : (at + 1) * third, : 2 * kv_width] for at in range(3)], axis=1
    )
    cut = third // 2
    extra_chunks = [
        jnp.concatenate([out_total, near_kv[:cut]], axis=0),
        jnp.concatenate([attn_total[:, 2 * kv_width :], near_kv[cut:]], axis=0),
    ]
    flow.leave(extra_chunks[1])
    flow.add(extra_chunks)
    flow.drain()

    if grad_down_w is None:
        grad_down_w = flow.settled(0, CHUNKS)
    grad_up_w = flow.settled(CHUNKS, CHUNKS)
    grad_gate_w = flow.settled(2 * CHUNKS, CHUNKS)
    with_out, with_query = (
        jnp.where(flow.line.is_end, *flow.line.pairs[3 * CHUNKS + at]).astype(F32) for at in range(2)
    )
    far_kv = jnp.concatenate([with_out[depth:], with_query[depth:]], axis=0)
    far_kv = jnp.concatenate(
        [far_kv[:, at * 2 * kv_width : (at + 1) * 2 * kv_width] for at in range(3)], axis=0
    )

    def own_part(row, size):
        return lax.dynamic_slice_in_dim(row, fsdp_index * size, size)

    return (
        output[None],
        grad_tokens[None],
        with_query[:depth],
        far_kv[:, :kv_width],
        far_kv[:, kv_width:],
        with_out[:depth],
        own_part(small_sums[2], depth),
        own_part(small_sums[3, :kv_width], kv_small),
        own_part(small_sums[3, kv_width : 2 * kv_width], kv_small),
        own_part(small_sums[0], depth),
        grad_gate_w.T,
        grad_up_w.T,
        grad_down_w,
        own_part(small_sums[1], depth),
    )


def solution(mesh):
    return jax.shard_map(
        shards,
        mesh=mesh,
        in_specs=(
            P("fsdp", "ctx", None),
            P("fsdp", "ctx", None),
            P("fsdp", None),
            P(),
            P("fsdp", None),
            P("fsdp", None),
            P("fsdp", None),
            P("fsdp", None),
            P("fsdp"),
            P("fsdp"),
            P("fsdp"),
            P("fsdp"),
            P(None, "fsdp"),
            P(None, "fsdp"),
            P("fsdp", None),
            P("fsdp"),
        ),
        out_specs=(
            P("fsdp", "ctx", None),
            P("fsdp", "ctx", None),
            P("fsdp", None),
            P("fsdp", None),
            P("fsdp", None),
            P("fsdp", None),
            P("fsdp"),
            P("fsdp"),
            P("fsdp"),
            P("fsdp"),
            P(None, "fsdp"),
            P(None, "fsdp"),
            P("fsdp", None),
            P("fsdp"),
        ),
        check_vma=False,
    )
```

```python
import functools

import jax
import jax.numpy as jnp
from jax import lax
from jax.experimental import pallas as pl
from jax.experimental.layout import Layout, with_layout_constraint
from jax.experimental.pallas import tpu as pltpu
from jax.sharding import PartitionSpec as P


HEAD = 128
CHUNKS = 5

THETA = 1000000.0
EPS = 1e-06
MASKED = -1e30
BF16 = jnp.bfloat16
F32 = jnp.float32


def dot_nn(left, right):
    return lax.dot_general(left, right, (((1,), (0,)), ((), ())), preferred_element_type=F32)


def dot_nt(left, right):
    return lax.dot_general(left, right, (((1,), (1,)), ((), ())), preferred_element_type=F32)


def shape_of(shape, dtype):
    return jax.ShapeDtypeStruct(shape, dtype)


VMEM = pl.BlockSpec(memory_space=pltpu.VMEM)


def room(mib):
    return pltpu.CompilerParams(vmem_limit_bytes=mib << 20)


def whole(shape):
    return pl.BlockSpec(shape, lambda *_: (0,) * len(shape))


def flat(value):
    return with_layout_constraint(value, Layout(major_to_minor=tuple(range(value.ndim))))


def exchange(value, axis, mask):
    count = lax.axis_size(axis)
    return flat(lax.ppermute(flat(value), axis, [(at, at ^ mask) for at in range(count)]))


def shift(value, axis, by):
    count = lax.axis_size(axis)
    return flat(lax.ppermute(flat(value), axis, [(at, (at + by) % count) for at in range(count)]))


def line_sum(piece, axis):
    count = lax.axis_size(axis)
    index = lax.axis_index(axis)
    piece = piece.astype(BF16)
    if count == 1:
        return piece
    if count % 2:
        return lax.psum(piece, axis)
    half = count // 2

    def plus(left, right):
        return (left.astype(F32) + right.astype(F32)).astype(BF16)

    for step in range(half - 1):
        pairs = [(step, step + 1), (count - 1 - step, count - 2 - step)]
        piece = plus(piece, lax.ppermute(piece, axis, pairs))
    piece = plus(piece, lax.ppermute(piece, axis, [(half - 1, half), (half, half - 1)]))
    for step in range(half - 1):
        low, high = half - 1 - step, half + step
        moved = lax.ppermute(piece, axis, [(low, low - 1), (high, high + 1)])
        piece = jnp.where((index == low - 1) | (index == high + 1), moved, piece)
    return piece


def turn(value, cosine, sine):
    return value * cosine + pltpu.roll(value, value.shape[-1] // 2, 1) * sine


SMEM = pl.BlockSpec(memory_space=pltpu.SMEM)


def assemble(index_ref, pieces, depth, out_ref, first):
    columns = out_ref.shape[1]
    for at, piece in enumerate(pieces):
        start = pl.multiple_of((index_ref[0] ^ at) * depth, 16)
        out_ref[pl.ds(start, depth), :] = piece[:depth, first : first + columns]


def prepare_kernel(count, depth, kv_depth, index_ref, tokens_ref, *refs):
    pieces = refs[:count]
    normed_ref, turned_ref, scale_ref, query_ref, kv_ref, attn_ref, ffn_ref = refs[count:]
    width = query_ref.shape[1]
    tall = 16
    lanes = -(-depth // HEAD) * HEAD
    kv_width = kv_depth * count
    vectors = jnp.zeros((tall, width), F32)
    bias = jnp.zeros((tall, kv_width), F32)
    lane = lax.broadcasted_iota(jnp.int32, (lanes, width), 0)
    column = lax.broadcasted_iota(jnp.int32, (lanes, width), 1)
    lane_kv = lax.broadcasted_iota(jnp.int32, (lanes, kv_width), 0)
    column_kv = lax.broadcasted_iota(jnp.int32, (lanes, kv_width), 1)
    for at in range(count):
        owner = index_ref[0] ^ at
        piece = pieces[at][depth : depth + tall, :lanes]
        pick = (column == lane + owner * depth) & (lane < depth)
        vectors = vectors + dot_nn(piece, jnp.where(pick, 1.0, 0.0).astype(BF16))
        pick = (column_kv == lane_kv + owner * kv_depth) & (lane_kv < kv_depth)
        bias = bias + dot_nn(piece, jnp.where(pick, 1.0, 0.0).astype(BF16))
    query_ref[...] = vectors[0:1, :]
    attn_ref[...] = vectors[3:4, :]
    ffn_ref[...] = vectors[4:5, :]
    kv_ref[:, :kv_width] = bias[1:2, :]
    kv_ref[:, kv_width:] = bias[2:3, :]
    hidden = tokens_ref[...].astype(F32)
    scale = lax.rsqrt(jnp.mean(hidden * hidden, axis=-1, keepdims=True) + EPS)
    normed = hidden * scale * vectors[3:4, :]
    scale_ref[...] = scale
    normed_ref[...] = normed.astype(BF16)
    turned_ref[...] = normed.T.astype(BF16)


def prepare(index, tokens, pieces, depth, kv_depth):
    rows, width = tokens.shape
    count = len(pieces)
    return pl.pallas_call(
        functools.partial(prepare_kernel, count, depth, kv_depth),
        in_specs=[SMEM] + [VMEM] * (1 + count),
        out_specs=[VMEM] * 7,
        out_shape=[
            shape_of((rows, width), BF16),
            shape_of((width, rows), BF16),
            shape_of((rows, 1), F32),
            shape_of((1, width), F32),
            shape_of((1, 2 * kv_depth * count), F32),
            shape_of((1, width), F32),
            shape_of((1, width), F32),
        ],
        compiler_params=room(12),
        name="prepare",
    )(index, tokens, *pieces)


def project_kernel(turned, count, depth, first, index_ref, normed_ref, *refs):
    pieces = refs[:count]
    bias_ref, cos_ref, sin_ref, out_ref, weight_ref = refs[count:]
    assemble(index_ref, pieces, depth, weight_ref, first)
    tile = 2 * HEAD
    for start in range(0, out_ref.shape[1], tile):
        part = slice(start, start + tile)
        raw = dot_nn(normed_ref[...], weight_ref[:, part]) + bias_ref[:, part]
        for at in range(2):
            value = raw[:, at * HEAD : (at + 1) * HEAD]
            place = start // HEAD + at
            if place < turned:
                value = turn(value, cos_ref[...], sin_ref[...])
            out_ref[:, place * HEAD : (place + 1) * HEAD] = value.astype(BF16)


def project(normed, pieces, depth, index, bias, cosine, sine, first, columns, turned):
    rows, width = normed.shape
    count = len(pieces)
    return pl.pallas_call(
        functools.partial(project_kernel, turned, count, depth, first),
        in_specs=[SMEM] + [VMEM] * (count + 4),
        out_specs=[VMEM] * 2,
        out_shape=[shape_of((rows, columns), BF16), shape_of((width, columns), BF16)],
        compiler_params=room(8),
        cost_estimate=pl.CostEstimate(
            flops=2 * rows * width * columns, bytes_accessed=4 * width * columns, transcendentals=0
        ),
        name="project",
    )(index, normed, *pieces, bias, cosine, sine)


def outer_rel_kernel(count, parts, index_ref, *refs):
    left_ref = refs[0]
    rights, outs = refs[1 : 1 + parts], refs[1 + parts :]
    depth = outs[0].shape[0]
    for which in range(count):
        rows = pl.ds(pl.multiple_of((index_ref[0] ^ which) * depth, 16), depth)
        left = left_ref[rows, :]
        start = 0
        for right in rights:
            outs[which][:, start : start + right.shape[1]] = dot_nn(left, right[...]).astype(BF16)
            start += right.shape[1]


def outer_rel(left, rights, index, count):
    width, rows = left.shape
    depth = width // count
    columns = sum(item.shape[1] for item in rights)
    return pl.pallas_call(
        functools.partial(outer_rel_kernel, count, len(rights)),
        in_specs=[SMEM] + [VMEM] * (1 + len(rights)),
        out_specs=[VMEM] * count,
        out_shape=[shape_of((depth, columns), BF16)] * count,
        compiler_params=room(12),
        cost_estimate=pl.CostEstimate(
            flops=2 * width * rows * columns, bytes_accessed=2 * width * columns, transcendentals=0
        ),
        name="outer_rel",
    )(index, left, *rights)


def join_kernel(count, depth, index_ref, mixed_ref, tokens_ref, gain_ref, *refs):
    pieces = refs[:count]
    mid_ref, normed_ref, scale_ref, weight_ref = refs[count:]
    assemble(index_ref, pieces, depth, weight_ref, 0)
    hidden = tokens_ref[...].astype(F32) + dot_nn(mixed_ref[...], weight_ref[...])
    mid_ref[...] = hidden
    scale = lax.rsqrt(jnp.mean(hidden * hidden, axis=-1, keepdims=True) + EPS)
    scale_ref[...] = scale
    normed_ref[...] = (hidden * scale * gain_ref[...]).astype(BF16)


def join(index, mixed, pieces, tokens, gain):
    rows, width = mixed.shape
    count = len(pieces)
    depth = pieces[0].shape[0]
    return pl.pallas_call(
        functools.partial(join_kernel, count, depth),
        in_specs=[SMEM] + [VMEM] * (3 + count),
        out_specs=[VMEM] * 4,
        out_shape=[
            shape_of((rows, width), F32),
            shape_of((rows, width), BF16),
            shape_of((rows, 1), F32),
            shape_of((width, width), BF16),
        ],
        compiler_params=room(12),
        cost_estimate=pl.CostEstimate(
            flops=2 * rows * width * width, bytes_accessed=2 * width * width, transcendentals=0
        ),
        name="join",
    )(index, mixed, tokens, gain, *pieces)


def part_kernel(count, *refs):
    terms = refs[:count]
    mid_ref, scale_ref, gain_ref, grad_ref, weight_ref = refs[count : count + 5]
    gm_ref, low_ref, gain_out, mixed_ref = refs[count + 5 :]
    total = terms[0][...].astype(F32)
    for item in terms[1:]:
        total = total + item[...].astype(F32)
    total = total.T
    hidden = mid_ref[...]
    scale = scale_ref[...]
    weighted = total * gain_ref[...]
    inner_mean = jnp.mean(weighted * hidden, axis=-1, keepdims=True)
    gain_out[...] = jnp.sum(total * (hidden * scale), axis=0, keepdims=True)
    grad = grad_ref[...].astype(F32) + scale * weighted - hidden * (scale * scale * scale * inner_mean)
    gm_ref[...] = grad
    low = grad.astype(BF16)
    low_ref[...] = low
    mixed_ref[...] = dot_nt(low, weight_ref[...]).astype(BF16)


def finish_kernel(count, *refs):
    terms, mid_ref, out_ref = refs[:count], refs[count], refs[count + 1]
    total = terms[0][...].astype(F32)
    for item in terms[1:]:
        total = total + item[...].astype(F32)
    out_ref[...] = (mid_ref[...] + total.T).astype(BF16)


def finish(terms, hidden_mid):
    rows, width = hidden_mid.shape
    return pl.pallas_call(
        functools.partial(finish_kernel, len(terms)),
        in_specs=[VMEM] * (len(terms) + 1),
        out_specs=VMEM,
        out_shape=shape_of((rows, width), BF16),
        compiler_params=room(12),
        cost_estimate=pl.CostEstimate(flops=0, bytes_accessed=16 * rows * width, transcendentals=0),
        name="finish",
    )(*terms, hidden_mid)


def part(terms, hidden_mid, scale, gain, grad_out, weight):
    rows, width = hidden_mid.shape
    return pl.pallas_call(
        functools.partial(part_kernel, len(terms)),
        in_specs=[VMEM] * (len(terms) + 5),
        out_specs=[VMEM] * 4,
        out_shape=[
            shape_of((rows, width), F32),
            shape_of((rows, width), BF16),
            shape_of((1, width), F32),
            shape_of((rows, width), BF16),
        ],
        compiler_params=room(16),
        cost_estimate=pl.CostEstimate(
            flops=2 * rows * width * width, bytes_accessed=2 * width * width + 20 * rows * width, transcendentals=0
        ),
        name="part",
    )(*terms, hidden_mid, scale, gain, grad_out, weight)


def fill_mask(bias_ref, key_ref, row_ref):
    keys = key_ref[...].T
    allowed = (keys[:, 0:1] <= row_ref[0:1, :]) & (keys[:, 1:2] == row_ref[1:2, :])
    bias_ref[...] = jnp.where(allowed, 0.0, MASKED)


def attend_kernel(
    group, scale, q_ref, k_ref, v_ref, key_ref, row_ref, out_ref, turned_ref, lse_ref, bias_ref
):
    @pl.when(pl.program_id(0) == 0)
    def _():
        fill_mask(bias_ref, key_ref, row_ref)

    key = k_ref[...]
    value_t = v_ref[...].T
    for at in range(group):
        query = q_ref[:, at * HEAD : (at + 1) * HEAD]
        scores = dot_nt(key, query) * scale + bias_ref[...]
        peak = jnp.max(scores, axis=0, keepdims=True)
        raised = jnp.exp(scores - peak)
        total = jnp.sum(raised, axis=0, keepdims=True)
        mixed = dot_nn(value_t, raised.astype(BF16)) / total
        turned_ref[at * HEAD : (at + 1) * HEAD, :] = mixed.astype(BF16)
        out_ref[:, at * HEAD : (at + 1) * HEAD] = mixed.T.astype(BF16)
        lse_ref[0, at : at + 1, :] = peak + jnp.log(total)


def attend(queries, every, marks, kv_heads):
    rows, width = queries.shape
    length = every.shape[0]
    wide = width // kv_heads
    group = wide // HEAD
    return pl.pallas_call(
        functools.partial(attend_kernel, group, HEAD ** (-0.5)),
        grid=(kv_heads,),
        in_specs=[
            pl.BlockSpec((rows, wide), lambda at: (0, at)),
            pl.BlockSpec((length, HEAD), lambda at: (0, at)),
            pl.BlockSpec((length, HEAD), lambda at: (0, at + kv_heads)),
        ]
        + [whole(item.shape) for item in marks],
        out_specs=[
            pl.BlockSpec((rows, wide), lambda at: (0, at)),
            pl.BlockSpec((wide, rows), lambda at: (at, 0)),
            pl.BlockSpec((1, group, rows), lambda at: (at, 0, 0)),
        ],
        out_shape=[
            shape_of((rows, width), BF16),
            shape_of((width, rows), BF16),
            shape_of((kv_heads, group, rows), F32),
        ],
        scratch_shapes=[pltpu.VMEM((length, rows), F32)],
        cost_estimate=pl.CostEstimate(
            flops=4 * rows * length * width * 4,
            bytes_accessed=4 * rows * width + 2 * every.size,
            transcendentals=rows * length * width // HEAD,
        ),
        compiler_params=room(24),
        name="attend",
    )(queries, every, every, *marks)


def attend_back_kernel(
    group,
    scale,
    q_ref,
    k_ref,
    v_ref,
    lse_ref,
    grad_ref,
    cos_ref,
    sin_ref,
    key_ref,
    row_ref,
    gq_ref,
    gk_ref,
    gv_ref,
    bias_ref,
):
    @pl.when(pl.program_id(0) == 0)
    def _():
        fill_mask(bias_ref, key_ref, row_ref)

    key = k_ref[...]
    value = v_ref[...]
    key_t = key.T
    grad_key = None
    grad_value = None
    for at in range(group):
        part = slice(at * HEAD, (at + 1) * HEAD)
        query = q_ref[:, part]
        grad = grad_ref[:, part]
        scores = dot_nt(key, query) * scale + bias_ref[...]
        probs = jnp.exp(scores - lse_ref[0, at : at + 1, :])
        grad_probs = dot_nt(value, grad)
        delta = jnp.sum(probs * grad_probs, axis=0, keepdims=True)
        grad_scores = (probs * (grad_probs - delta) * scale).astype(BF16)
        value_term = dot_nn(probs.astype(BF16), grad)
        key_term = dot_nn(grad_scores, query)
        grad_value = value_term if grad_value is None else grad_value + value_term
        grad_key = key_term if grad_key is None else grad_key + key_term
        grad_query = dot_nn(key_t, grad_scores).T
        gq_ref[:, part] = turn(grad_query, cos_ref[...], -sin_ref[...]).astype(BF16)
    gk_ref[...] = grad_key.astype(BF16)
    gv_ref[...] = grad_value.astype(BF16)


def attend_back(queries, every, lse, grad_mixed, cosine, sine, marks, kv_heads):
    rows, width = queries.shape
    length = every.shape[0]
    wide = width // kv_heads
    group = wide // HEAD
    by_group = pl.BlockSpec((rows, wide), lambda at: (0, at))
    by_head = pl.BlockSpec((length, HEAD), lambda at: (0, at))
    return pl.pallas_call(
        functools.partial(attend_back_kernel, group, HEAD ** (-0.5)),
        grid=(kv_heads,),
        in_specs=[
            by_group,
            by_head,
            pl.BlockSpec((length, HEAD), lambda at: (0, at + kv_heads)),
            pl.BlockSpec((1, group, rows), lambda at: (at, 0, 0)),
            by_group,
            whole(cosine.shape),
            whole(sine.shape),
        ]
        + [whole(item.shape) for item in marks],
        out_specs=[by_group, by_head, by_head],
        out_shape=[
            shape_of((rows, width), BF16),
            shape_of((length, kv_heads * HEAD), BF16),
            shape_of((length, kv_heads * HEAD), BF16),
        ],
        scratch_shapes=[pltpu.VMEM((length, rows), F32)],
        cost_estimate=pl.CostEstimate(
            flops=10 * rows * length * width * 3,
            bytes_accessed=8 * rows * width + 4 * every.size,
            transcendentals=rows * length * width // HEAD,
        ),
        compiler_params=room(32),
        name="attend_back",
    )(queries, every, every, lse, grad_mixed, cosine, sine, *marks)


def flip_kernel(*refs):
    count = len(refs) // 2
    for at in range(count):
        refs[count + at][...] = refs[at][...].T


def flip(*arrays):
    deep, wide = arrays[0].shape
    tile = 256
    return pl.pallas_call(
        flip_kernel,
        grid=(wide // tile,),
        in_specs=[pl.BlockSpec((deep, tile), lambda at: (0, at))] * len(arrays),
        out_specs=[pl.BlockSpec((tile, deep), lambda at: (at, 0))] * len(arrays),
        out_shape=[shape_of((wide, deep), item.dtype) for item in arrays],
        cost_estimate=pl.CostEstimate(flops=0, bytes_accessed=4 * len(arrays) * deep * wide, transcendentals=0),
        compiler_params=room(20),
        name="flip",
    )(*arrays)


def feed_kernel(x_ref, c_ref, gate_ref, up_ref, down_ref, inner_ref, gg_ref, gu_ref):
    units = gate_ref.shape[0]
    step = units // 2
    for start in range(0, units, step):
        unit = slice(start, start + step)
        gate = dot_nt(gate_ref[unit, :], x_ref[...])
        upper = dot_nt(up_ref[unit, :], x_ref[...])
        grad = dot_nt(down_ref[unit, :], c_ref[...])
        half = 0.5 * jnp.tanh(0.5 * gate)
        sigma = half + 0.5
        smooth = gate * sigma
        inner_ref[unit, :] = (smooth * upper).astype(BF16)
        gu_ref[unit, :] = (grad * smooth).astype(BF16)
        gg_ref[unit, :] = (grad * upper * (sigma + smooth * (0.5 - half))).astype(BF16)


def feed(x, c, gate_t, up_t, w_down):
    rows, width = x.shape
    units = gate_t.shape[0]
    return pl.pallas_call(
        feed_kernel,
        in_specs=[VMEM] * 5,
        out_specs=[VMEM] * 3,
        out_shape=[shape_of((units, rows), BF16)] * 3,
        compiler_params=room(8),
        cost_estimate=pl.CostEstimate(
            flops=6 * rows * width * units,
            bytes_accessed=4 * rows * width + 6 * rows * units,
            transcendentals=rows * units,
        ),
        name="feed",
    )(x, c, gate_t, up_t, w_down)


def back_kernel(count, *refs):
    weights, grads, out_ref = refs[:count], refs[count : 2 * count], refs[2 * count]
    width = weights[0].shape[0]
    tile = width // 2
    for start in range(0, width, tile):
        part = slice(start, start + tile)
        total = None
        for weight, grad in zip(weights, grads):
            term = dot_nn(weight[part, :], grad[...])
            total = term if total is None else total + term
        out_ref[part, :] = total.astype(BF16)


def back(weights, grads):
    count = len(weights)
    width, units = weights[0].shape
    rows = grads[0].shape[1]
    return pl.pallas_call(
        functools.partial(back_kernel, count),
        in_specs=[VMEM] * (2 * count),
        out_specs=VMEM,
        out_shape=shape_of((width, rows), BF16),
        compiler_params=room(8),
        cost_estimate=pl.CostEstimate(
            flops=2 * count * rows * width * units,
            bytes_accessed=2 * count * (width + rows) * units,
            transcendentals=0,
        ),
        name="back",
    )(*weights, *grads)


def outer_kernel(pieces, first, *refs):
    lefts, rights, outs = refs[:pieces], refs[pieces : 2 * pieces], refs[2 * pieces :]
    size, width = outs[0].shape
    units = slice(first * size, (first + len(outs)) * size)
    tile = 512
    for start in range(0, width, tile):
        part = slice(start, start + tile)
        total = None
        for left, right in zip(lefts, rights):
            term = dot_nn(left[units, :], right[:, part])
            total = term if total is None else total + term
        for at, out in enumerate(outs):
            out[:, part] = total[at * size : (at + 1) * size, :].astype(BF16)


def outer(lefts, rights, first, stop):
    units, rows = lefts[0].shape
    width = rights[0].shape[1]
    pieces = len(lefts)
    size = units // CHUNKS
    chunks = stop - first
    return pl.pallas_call(
        functools.partial(outer_kernel, pieces, first),
        in_specs=[VMEM] * (2 * pieces),
        out_specs=[VMEM] * chunks,
        out_shape=[shape_of((size, width), BF16)] * chunks,
        compiler_params=room(8),
        cost_estimate=pl.CostEstimate(
            flops=2 * chunks * size * rows * pieces * width,
            bytes_accessed=2 * pieces * (units * rows + rows * width),
            transcendentals=0,
        ),
        name="outer",
    )(*lefts, *rights)


def settle_kernel(count, end_ref, *refs):
    got, sent, out_ref = refs[:count], refs[count : 2 * count], refs[-1]
    size = got[0].shape[0]

    @pl.when(end_ref[0] == 1)
    def _():
        for at in range(count):
            out_ref[at * size : (at + 1) * size, :] = got[at][...].astype(F32)

    @pl.when(end_ref[0] == 0)
    def _():
        for at in range(count):
            out_ref[at * size : (at + 1) * size, :] = sent[at][...].astype(F32)


def settle(is_end, pairs, first, total, held):
    count = len(pairs)
    size, width = pairs[0][0].shape
    tile = 256
    block = pl.BlockSpec((size, tile), lambda at, end: (0, at))
    extra = [] if held is None else [held]
    return pl.pallas_call(
        functools.partial(settle_kernel, count),
        grid_spec=pltpu.PrefetchScalarGridSpec(
            num_scalar_prefetch=1,
            grid=(width // tile,),
            in_specs=[block] * (2 * count) + [pl.BlockSpec(memory_space=pl.ANY)] * len(extra),
            out_specs=pl.BlockSpec((count * size, tile), lambda at, end: (first // count, at)),
        ),
        out_shape=shape_of((total * size, width), F32),
        input_output_aliases={1 + 2 * count: 0} if extra else {},
        compiler_params=room(16),
        cost_estimate=pl.CostEstimate(flops=0, bytes_accessed=8 * count * size * width, transcendentals=0),
        name="settle",
    )(is_end.astype(jnp.int32).reshape(1), *[item[0] for item in pairs], *[item[1] for item in pairs], *extra)


def tie(values, *others):
    return lax.optimization_barrier((values, others))[0]


class Line:
    LAG = 3

    def __init__(self, axis):
        self.axis = axis
        index = lax.axis_index(axis)
        self.is_end = (index == 0) | (index == lax.axis_size(axis) - 1)
        self.simple = lax.axis_size(axis) != 4
        self.chunks, self.mine, self.theirs, self.pairs = [], {}, {}, {}
        self.moving = {}
        self.closed = False
        self.started = self.taken = 0

    def outward(self, token):
        at, old = self.started, self.started - self.LAG
        if self.simple or (at >= len(self.chunks) and not (self.closed and old < len(self.chunks))):
            return token
        if old < 0:
            value = self.chunks[at]
        else:
            theirs = tie(self.theirs[old], token)
            value = (self.mine[old].astype(F32) + theirs.astype(F32)).astype(BF16)
            if at < len(self.chunks):
                value = jnp.where(self.is_end, self.chunks[at], value)
        moved = flat(lax.ppermute(flat(value), self.axis, [(0, 1), (1, 0), (2, 3), (3, 2)]))
        self.moving[at] = (value, moved)
        self.started += 1
        return value

    def inward(self, token):
        if self.simple or self.taken >= self.started:
            return token
        at = self.taken
        value, got = self.moving.pop(at)
        got = tie(got, token)
        if at >= self.LAG:
            self.pairs[at - self.LAG] = (got, value)
        self.taken += 1
        if at >= len(self.chunks):
            return got
        mine = (self.chunks[at].astype(F32) + got.astype(F32)).astype(BF16)
        self.mine[at] = mine
        self.theirs[at] = self.swap(mine)
        return mine

    def swap(self, value):
        wide = lax.axis_size("fsdp")
        pairs = []
        for at, other in enumerate((None, 2, 1, None)):
            for near in range(wide):
                to = at * wide + (near ^ 1) if other is None else other * wide + near
                pairs.append((at * wide + near, to))
        return flat(lax.ppermute(flat(value), (self.axis, "fsdp"), pairs))


class Flow:
    def __init__(self, axis):
        self.token = None
        self.line = Line(axis)

    def enter(self, values):
        return values if self.token is None else tie(values, self.token)

    def leave(self, token):
        self.token = token

    def out(self):
        self.token = self.line.outward(self.token)

    def take(self):
        self.token = self.line.inward(self.token)

    def both(self):
        self.out()
        self.take()

    def add(self, chunks):
        self.line.chunks.extend(chunks)

    def drain(self):
        line = self.line
        line.closed = True
        if line.simple:
            sums = [line_sum(chunk, line.axis) for chunk in line.chunks]
            line.pairs = {at: (value, value) for at, value in enumerate(sums)}
            return
        while line.started < len(line.chunks) + line.LAG:
            self.both()
        while line.taken < line.started:
            self.take()

    def settled(self, first, count, held=None, start=0, stop=None):
        pairs = [self.line.pairs[first + at] for at in range(start, stop or count)]
        return settle(self.line.is_end, pairs, start, count, held)


def rotary_tables(places, head):
    half = head // 2
    freqs = THETA ** (-jnp.arange(half, dtype=jnp.float32) / half)
    angles = places.astype(jnp.float32)[:, None] * freqs[None, :]
    cosine, sine = jnp.cos(angles), jnp.sin(angles)
    return jnp.concatenate([cosine, cosine], axis=1), jnp.concatenate([-sine, sine], axis=1)


def norm_backward(hidden, scale_rows, gain, grad_normed):
    weighted = grad_normed * gain
    inner_mean = jnp.mean(weighted * hidden, axis=-1, keepdims=True)
    grad_hidden = scale_rows * weighted - hidden * scale_rows * scale_rows * scale_rows * inner_mean
    grad_gain = jnp.sum(grad_normed * hidden * scale_rows, axis=0)
    return (grad_hidden, grad_gain)


def turn_rows(value, cosine, sine):
    rows = value.shape[0]
    heads = value.reshape(rows, -1, HEAD)
    half = HEAD // 2
    swapped = jnp.concatenate([heads[..., half:], heads[..., :half]], axis=-1)
    return (heads * cosine[:, None, :] + swapped * sine[:, None, :]).reshape(value.shape)


def shards(
    tokens,
    cotangent,
    doc_ids,
    block_order,
    w_query,
    w_key,
    w_value,
    w_out,
    b_query,
    b_key,
    b_value,
    gain_attn,
    w_gate,
    w_up,
    w_down,
    gain_ffn,
):
    ctx_count = lax.axis_size("ctx")
    ctx_index = lax.axis_index("ctx")
    fsdp_count = lax.axis_size("fsdp")
    rows = tokens.shape[1]
    width = tokens.shape[2]
    depth = w_query.shape[0]
    block = rows // 2
    kv_width = w_key.shape[1]
    kv_heads = kv_width // HEAD

    grad_out = cotangent[0]
    fsdp_index = lax.axis_index("fsdp")
    index = fsdp_index.astype(jnp.int32).reshape(1)

    evens = list(range(2, fsdp_count, 2))
    slots = [(0, 1)]
    for at in range(0, len(evens), 2):
        near = evens[at : at + 2]
        if len(near) == 2:
            slots.append(tuple(near))
            slots.append(tuple(mask ^ 1 for mask in near))
        else:
            slots.append((near[0], near[0] ^ 1))
    order = [mask for pair in slots for mask in pair]

    def far(value, mask, got):
        if mask == 6 and fsdp_count == 8:
            cut = value.shape[0] // 2
            return jnp.concatenate(
                [exchange(got[2][:cut], "fsdp", 4), exchange(got[4][cut:], "fsdp", 2)], axis=0
            )
        return exchange(value, "fsdp", mask)

    kv_small = kv_width // fsdp_count
    vectors = [b_query, b_key, b_value, gain_attn, gain_ffn]
    columns = 2 * kv_width + width
    small = jnp.stack([jnp.pad(item, (0, columns - item.shape[0])) for item in vectors], axis=0)
    small = jnp.pad(small, ((0, 16 - len(vectors)), (0, 0)))
    w_near = jnp.concatenate([jnp.concatenate([w_key, w_value, w_query], axis=1), small], axis=0)
    w_of = {0: w_near}
    for mask in evens[:2]:
        w_of[mask] = exchange(w_near, "fsdp", mask)

    blocks = jnp.stack([block_order, 2 * ctx_count - 1 - block_order], axis=1).reshape(-1)
    places = (blocks[:, None] * block + jnp.arange(block, dtype=jnp.int32)[None, :]).reshape(-1)
    own_places = lax.dynamic_slice_in_dim(places, ctx_index * rows, rows)
    key_docs = doc_ids[0]
    own_docs = lax.dynamic_slice_in_dim(key_docs, ctx_index * rows, rows)

    def mark(*values):
        marked = jnp.stack([item.astype(F32) for item in values], axis=0)
        return jnp.pad(marked, ((0, 8 - len(values)), (0, 0)))

    marks = (mark(places, key_docs), mark(own_places, own_docs))
    cosine, sine = rotary_tables(own_places, HEAD)

    tokens_low = tokens[0]
    hidden = tokens_low.astype(F32)
    gate_t, up_t = w_gate.T, w_up.T
    gate_r, up_r, down_r = flip(gate_t, up_t, tie(w_down, cosine, sine, marks))

    got = tie([w_of[mask] for mask in evens[:2]], gate_r)
    for mask, value in zip(evens[:2], got):
        w_of[mask] = value
    for mask in evens[2:]:
        w_of[mask] = far(w_near, mask, w_of)
    for mask in [0] + evens:
        w_of[mask ^ 1] = exchange(w_of[mask], "fsdp", 1)
    w_parts = [w_of[mask] for mask in range(fsdp_count)]
    o_of = {0: w_out}
    o_near = tie(w_out, [w_of[mask] for mask in evens[2:]])
    for mask in evens:
        o_of[mask] = exchange(o_near, "fsdp", mask)
    normed, normed_t, scale_one, query_bias, kv_bias, attn_gain, ffn_gain = prepare(
        index, tokens_low, w_parts, depth, kv_small
    )
    keys_values, w_kv_all = project(
        normed, w_parts, depth, index, kv_bias, cosine, sine, 0, 2 * kv_width, kv_heads
    )
    every = jnp.zeros((ctx_count, rows, 2 * kv_width), BF16)
    for by in range(ctx_count):
        moved = shift(keys_values, "ctx", by) if by else keys_values
        origin = (ctx_index - by) % ctx_count
        every = lax.dynamic_update_slice(every, moved[None], (origin, 0, 0))
    every = every.reshape(ctx_count * rows, 2 * kv_width)
    queries, w_q_all = project(
        normed, w_parts, depth, index, query_bias, cosine, sine, 2 * kv_width, width, width // HEAD
    )
    got = tie([o_of[mask] for mask in evens], queries)
    for mask, value in zip(evens, got):
        o_of[mask] = value
    for mask in [0] + evens:
        o_of[mask ^ 1] = exchange(o_of[mask], "fsdp", 1)
    o_parts = [o_of[mask] for mask in range(fsdp_count)]

    c_near = tie(grad_out, got)
    c_of = {0: grad_out}
    for mask in evens:
        c_of[mask] = exchange(c_near, "fsdp", mask)
    mixed, mixed_t, lse = attend(queries, every, marks, kv_heads)
    got = tie([c_of[mask] for mask in evens], mixed)
    for mask, value in zip(evens, got):
        c_of[mask] = value
    for mask in [0] + evens:
        c_of[mask ^ 1] = exchange(c_of[mask], "fsdp", 1)
    hidden_mid, normed_two, scale_two, out_all = join(index, mixed, o_parts, tokens_low, ffn_gain)

    x_of = {0: normed_two, 1: exchange(normed_two, "fsdp", 1)}
    for mask in evens[:2]:
        x_of[mask] = exchange(normed_two, "fsdp", mask)
    inner, grad_gate, grad_upper = {}, {}, {}
    last = None
    for slot, mask in enumerate(order):
        if slot == 2:
            got = tie([x_of[mask] for mask in evens[:2]], last)
            for other, value in zip(evens[:2], got):
                x_of[other] = value
            for other in evens[2:]:
                x_of[other] = far(normed_two, other, x_of)
            for other in evens[:2]:
                x_of[other ^ 1] = exchange(x_of[other], "fsdp", 1)
        if slot == 5:
            got = tie([x_of[other] for other in evens[2:]], last)
            for other, value in zip(evens[2:], got):
                x_of[other] = value
                x_of[other ^ 1] = exchange(value, "fsdp", 1)
        value = x_of[mask] if last is None else tie(x_of[mask], last)
        last, gg, gu = feed(value, c_of[mask], gate_t, up_t, w_down)
        inner[mask], grad_gate[mask], grad_upper[mask] = last, gg, gu
    gate_r, up_r, down_r = tie((gate_r, up_r, down_r), last)
    x_parts = [x_of[mask] for mask in order]
    c_parts = [c_of[mask] for mask in order]

    def in_order(of):
        return [of[mask] for mask in order]

    flow = Flow("ctx")

    def grads_back(mask):
        value = back([gate_r, up_r], flow.enter([grad_gate[mask], grad_upper[mask]]))
        flow.leave(value)
        return value

    def rows_down(mask):
        value = back([down_r], flow.enter([inner[mask]]))
        flow.leave(value)
        return value

    def pair_up(terms, mask):
        return terms[mask], exchange(terms[mask ^ 1], "fsdp", 1)

    def pairs_of(terms, pairs):
        for mask in [0] + evens:
            if mask in terms and mask ^ 1 in terms and mask not in pairs:
                pairs[mask] = pair_up(terms, mask)

    def pair_sum(pair):
        return pair[0].astype(F32) + pair[1].astype(F32)

    def far_sums(pairs):
        masks = sorted((mask for mask in pairs if mask), reverse=True)
        near = flow.enter([pairs[mask] for mask in masks])
        sums = [pair_sum(pair).astype(BF16) for pair in near]
        flow.leave(sums[-1])
        return [exchange(value, "fsdp", mask) for mask, value in zip(masks, sums)]

    def gather_up(own, moved):
        total = pair_sum(own)
        for value in moved:
            total = total + value.astype(F32)
        return total

    def work(lefts, rights, first, stop):
        chunks = outer(flow.enter(lefts), rights, first, stop)
        flow.leave(chunks[0])
        flow.add(chunks)

    def backs(masks, terms, pairs):
        for mask in masks:
            terms[mask] = grads_back(mask)
        pairs_of(terms, pairs)

    def downs(masks, terms, pairs):
        for mask in masks:
            terms[mask] = rows_down(mask)
        pairs_of(terms, pairs)

    late = [mask for mask in reversed(order[2:])]
    middle = (len(late) - 2) // 2 + 2
    first = 2
    terms, pairs = {}, {}
    downed, upped, gated = in_order(inner), in_order(grad_upper), in_order(grad_gate)
    work(downed, c_parts, 0, first)
    flow.out()
    work(downed, c_parts, first, CHUNKS)
    backs(late[:2], terms, pairs)
    flow.out()
    backs(late[2:middle], terms, pairs)
    flow.take()
    backs(late[middle:], terms, pairs)
    flow.out()
    moved = far_sums(pairs)
    flow.take()
    backs((1, 0), terms, pairs)
    flow.out()
    work(upped, x_parts, 0, first)
    flow.take()
    work(upped, x_parts, first, CHUNKS)
    flow.out()
    work(gated, x_parts, 0, first)
    flow.take()
    work(gated, x_parts, first, CHUNKS)
    flow.out()
    out_terms, out_pairs = {}, {}
    downs(late[:middle], out_terms, out_pairs)
    flow.take()
    downs(late[middle:] + [1, 0], out_terms, out_pairs)
    flow.out()
    own_pair, moved = flow.enter((pairs[0], moved))
    grad_mid, grad_mid_low, grad_gain_ffn, grad_mixed = part(
        [*own_pair, *moved], hidden_mid, scale_two, ffn_gain, grad_out, out_all
    )
    flow.leave(grad_mixed)
    flow.take()
    out_moved = far_sums(out_pairs)
    flow.out()
    grad_query_pre, grad_keys, grad_values = attend_back(
        queries, every, lse, flow.enter(grad_mixed), cosine, sine, marks, kv_heads
    )
    flow.leave(grad_query_pre)
    flow.take()
    grad_keys, grad_values = flow.enter((grad_keys, grad_values))
    own_parts = []
    for mask in range(ctx_count):
        start = (ctx_index ^ mask) * rows
        own_parts.append(
            jnp.concatenate(
                [
                    lax.dynamic_slice_in_dim(grad_keys, start, rows),
                    lax.dynamic_slice_in_dim(grad_values, start, rows),
                ],
                axis=1,
            )
        )
    halving = [1 << at for at in range(ctx_count.bit_length() - 1)]

    def halve(mask):
        keep = [at for at in range(len(own_parts)) if own_parts[at] is not None and not at & mask]
        return {at: exchange(own_parts[at | mask], "ctx", mask) for at in keep}

    def halved(moved, mask):
        moved = flow.enter(moved)
        for at, value in moved.items():
            own_parts[at] = (own_parts[at].astype(F32) + value.astype(F32)).astype(BF16)
            own_parts[at | mask] = None
        flow.leave(own_parts[0])

    part_moved = halve(halving[0])
    flow.leave(own_parts[0])
    flow.out()
    out_pieces = outer_rel(mixed_t, [flow.enter(grad_mid_low)], index, fsdp_count)
    flow.leave(out_pieces[0])
    attn_out_pairs = {}
    pairs_of(dict(enumerate(out_pieces)), attn_out_pairs)
    flow.take()
    attn_out_moved = far_sums(attn_out_pairs)
    for at, mask in enumerate(halving):
        halved(part_moved, mask)
        if at + 1 < len(halving):
            part_moved = halve(halving[at + 1])
            flow.both()
    own_out, out_moved = flow.enter((out_pairs[0], out_moved))
    output = finish([*own_out, *out_moved], hidden_mid)
    flow.leave(output)
    own_grad = own_parts[0].astype(F32)
    grad_key_pre = turn_rows(own_grad[:, :kv_width], cosine, -sine).astype(BF16)
    grad_value_pre = own_grad[:, kv_width:].astype(BF16)
    grad_kv_pre = jnp.concatenate([grad_key_pre, grad_value_pre], axis=1)
    flow.leave(grad_kv_pre)
    attn_pieces = outer_rel(
        normed_t, [flow.enter(grad_kv_pre), grad_query_pre], index, fsdp_count
    )
    flow.leave(attn_pieces[0])
    attn_pairs = {}
    pairs_of(dict(enumerate(attn_pieces)), attn_pairs)
    flow.out()
    attn_moved = far_sums(attn_pairs)
    flow.take()
    grad_kv_pre = flow.enter(grad_kv_pre)
    grad_normed = jnp.einsum("te,de->td", grad_kv_pre, w_kv_all, preferred_element_type=F32)
    grad_normed = grad_normed + jnp.einsum(
        "te,de->td", grad_query_pre, w_q_all, preferred_element_type=F32
    )
    grad_norm_one, grad_gain_attn = norm_backward(hidden, scale_one, attn_gain, grad_normed)
    grad_tokens = (grad_mid + grad_norm_one).astype(BF16)
    grad_bias = jnp.sum(grad_kv_pre.astype(F32), axis=0)
    small_sums = jnp.stack(
        [
            grad_gain_attn,
            grad_gain_ffn.reshape(-1),
            jnp.sum(grad_query_pre.astype(F32), axis=0),
            jnp.pad(grad_bias, (0, width - 2 * kv_width)),
        ],
        axis=0,
    )
    small_sums = jnp.pad(small_sums, ((0, 4), (0, 0)))
    flow.leave(small_sums)
    steps = [("ctx", 1 << at) for at in range(ctx_count.bit_length() - 1)]
    steps += [("fsdp", 1 << at) for at in range(fsdp_count.bit_length() - 1)]
    other = exchange(small_sums, *steps[0])

    def add_small(step):
        nonlocal small_sums, other
        small_sums = small_sums + flow.enter(other)
        flow.leave(small_sums)
        if step + 1 < len(steps):
            other = exchange(small_sums, *steps[step + 1])

    flow.both()
    flow.both()
    add_small(0)
    flow.both()
    add_small(1)
    attn_own, attn_moved, out_own, attn_out_moved = flow.enter(
        (attn_pairs[0], attn_moved, attn_out_pairs[0], attn_out_moved)
    )
    attn_total = gather_up(attn_own, attn_moved).astype(BF16)
    out_total = gather_up(out_own, attn_out_moved).astype(BF16)
    third = depth // 3
    near_kv = jnp.concatenate(
        [attn_total[at * third : (at + 1) * third, : 2 * kv_width] for at in range(3)], axis=1
    )
    cut = third // 2
    extra_chunks = [
        jnp.concatenate([out_total, near_kv[:cut]], axis=0),
        jnp.concatenate([attn_total[:, 2 * kv_width :], near_kv[cut:]], axis=0),
    ]
    flow.leave(extra_chunks[1])
    flow.add(extra_chunks)
    for step in range(2, len(steps)):
        flow.both()
        add_small(step)
    flow.drain()

    grad_down_w = flow.settled(0, CHUNKS)
    grad_up_w = flow.settled(CHUNKS, CHUNKS)
    grad_gate_w = flow.settled(2 * CHUNKS, CHUNKS)
    with_out, with_query = (
        jnp.where(flow.line.is_end, *flow.line.pairs[3 * CHUNKS + at]).astype(F32) for at in range(2)
    )
    far_kv = jnp.concatenate([with_out[depth:], with_query[depth:]], axis=0)
    far_kv = jnp.concatenate(
        [far_kv[:, at * 2 * kv_width : (at + 1) * 2 * kv_width] for at in range(3)], axis=0
    )

    def own_part(row, size):
        return lax.dynamic_slice_in_dim(row, fsdp_index * size, size)

    return (
        output[None],
        grad_tokens[None],
        with_query[:depth],
        far_kv[:, :kv_width],
        far_kv[:, kv_width:],
        with_out[:depth],
        own_part(small_sums[2], depth),
        own_part(small_sums[3, :kv_width], kv_small),
        own_part(small_sums[3, kv_width : 2 * kv_width], kv_small),
        own_part(small_sums[0], depth),
        grad_gate_w.T,
        grad_up_w.T,
        grad_down_w,
        own_part(small_sums[1], depth),
    )


def solution(mesh):
    return jax.shard_map(
        shards,
        mesh=mesh,
        in_specs=(
            P("fsdp", "ctx", None),
            P("fsdp", "ctx", None),
            P("fsdp", None),
            P(),
            P("fsdp", None),
            P("fsdp", None),
            P("fsdp", None),
            P("fsdp", None),
            P("fsdp"),
            P("fsdp"),
            P("fsdp"),
            P("fsdp"),
            P(None, "fsdp"),
            P(None, "fsdp"),
            P("fsdp", None),
            P("fsdp"),
        ),
        out_specs=(
            P("fsdp", "ctx", None),
            P("fsdp", "ctx", None),
            P("fsdp", None),
            P("fsdp", None),
            P("fsdp", None),
            P("fsdp", None),
            P("fsdp"),
            P("fsdp"),
            P("fsdp"),
            P("fsdp"),
            P(None, "fsdp"),
            P(None, "fsdp"),
            P("fsdp", None),
            P("fsdp"),
        ),
        check_vma=False,
    )
```
